512 devices in a mesh: level: 16 (over z_lo, core), space: 32 (over x, z_hi, y).
Axes of the slice: x: 4, y: 4, z: 16 (z_hi: 2, z_lo: 8; z = z_hi * 8 + z_lo), core: 2. Of those that a mesh axis runs over, the one named last changes fastest.
Arguments:
- fc_long: bfloat16 [704, 16, 8, 3, 1440], P('space', 'level'), may hold values from -6 to 6
- fc_short: bfloat16 [704, 16, 8, 3, 1440], P('space', 'level'), may hold values from -6 to 6
Outputs:
- cross: float32 [2, 3, 16, 16, 448, 384], P(None, None, 'level', None, 'space')
The draws below stay inside these ranges and needn't reach their ends.
All inputs are finite; a program needn't handle non-finite values.
Results may differ from the reference program's by a relative error of at most 0.0077.
Values may be sent and summed in bfloat16 or wider, within the bound.
No kernel may reach another device: no remote copies, remote signals or barrier semaphores. Data moves between devices by JAX's collectives and lax.ppermute only.
A program may use at most 64 MiB of HBM per device.

```python
import math
import jax
import jax.numpy as jnp
from jax import lax

LON = 1440
LAT = 704
MK = 448
NL = 384
V = 3
S = 8
L = 16


def shard_levels(own_key, dims, split, smallest, top_value):
    def one(dim, blocks):
        draws = jax.random.uniform(jax.random.fold_in(jax.random.fold_in(own_key, 6), dim), (blocks,), jnp.float32, smallest / len(split), top_value / len(split))
        return jnp.repeat(jnp.exp(draws), dims[dim] // blocks).reshape((-1,) + (1,) * (len(dims) - dim - 1))

    gain = one(*split[0])
    for cut in split[1:]:
        gain = gain * one(*cut)
    return gain


def normal_values(stream_key, dims, deviation, most, pieces=(), kind=jnp.bfloat16):
    factor_of = shard_levels(stream_key, dims, pieces, -0.22, 0.18) if pieces else 1.0
    result = jax.random.normal(stream_key, dims, jnp.float32) * deviation * factor_of
    return jnp.minimum(jnp.maximum(result, -most), most).astype(kind)


def setup_inputs(seed: int = 0) -> dict:
    seeds = jax.random.split(jax.random.key(seed), 3)
    fc_long = normal_values(seeds[0], (LAT, L, S, V, LON), 1.0, 6.0, ((0, 32), (1, 16)))
    fc_short = normal_values(seeds[1], (LAT, L, S, V, LON), 1.0, 6.0, ((0, 32), (1, 16)))
    return {"fc_long": fc_long, "fc_short": fc_short}


def zonal_table(lon_size, wave_total, space_size):
    wave_local = wave_total // space_size
    lon_index = jnp.arange(lon_size, dtype=jnp.int32)[:, None, None]
    wave_index = (jnp.arange(space_size, dtype=jnp.int32)[:, None] * wave_local + jnp.arange(wave_local, dtype=jnp.int32)[None, :])[None]
    phase_int = lon_index * wave_index % lon_size
    angle_rad = 2.0 * math.pi / lon_size * phase_int.astype(jnp.float32)
    table = jnp.stack([jnp.cos(angle_rad), -jnp.sin(angle_rad)], axis=2) / math.sqrt(lon_size)
    return table.astype(jnp.bfloat16)

def merid_table(lat_size, wave_total):
    lat_index = jnp.arange(lat_size, dtype=jnp.int32)[:, None]
    wave_index = jnp.arange(wave_total, dtype=jnp.int32)[None, :] - wave_total // 2
    phase_int = lat_index * wave_index % lat_size
    angle_rad = 2.0 * math.pi / lat_size * phase_int.astype(jnp.float32)
    table = jnp.stack([jnp.cos(angle_rad), jnp.sin(angle_rad)], axis=1) / math.sqrt(lat_size)
    return table.astype(jnp.bfloat16)

def cross_pair(own_spec, other_spec):
    own_spec = own_spec.astype(jnp.float32)
    other_spec = other_spec.astype(jnp.float32)
    pattern = 'savkl,sbvkl->vabkl'
    highest = lax.Precision.HIGHEST
    co_spec = jnp.einsum(pattern, own_spec[0], other_spec[0], precision=highest) + jnp.einsum(pattern, own_spec[1], other_spec[1], precision=highest)
    quad_spec = jnp.einsum(pattern, own_spec[1], other_spec[0], precision=highest) - jnp.einsum(pattern, own_spec[0], other_spec[1], precision=highest)
    return jnp.stack([co_spec, quad_spec]) / own_spec.shape[1]

def reference(fc_long, fc_short):
    diff_field = (fc_long.astype(jnp.float32) - fc_short.astype(jnp.float32)).astype(jnp.bfloat16)
    zonal_tab = zonal_table(LON, MK, 1)[:, 0].astype(jnp.float32)
    merid_tab = merid_table(LAT, NL).astype(jnp.float32)
    highest = lax.Precision.HIGHEST

    def level_spec(lev_field):
        zonal_coeff = jnp.einsum('ysvx,xuk->ysvuk', lev_field.astype(jnp.float32), zonal_tab, precision=highest).astype(jnp.bfloat16)
        products = jnp.einsum('ysvuk,ytl->svuktl', zonal_coeff.astype(jnp.float32), merid_tab, precision=highest)
        real_part = products[:, :, 0, :, 0, :] + products[:, :, 1, :, 1, :]
        imag_part = products[:, :, 1, :, 0, :] - products[:, :, 0, :, 1, :]
        return jnp.stack([real_part, imag_part]).astype(jnp.bfloat16)
    spectra = lax.map(level_spec, jnp.moveaxis(diff_field, 1, 0))
    spectra = jnp.transpose(spectra, (1, 2, 0, 3, 4, 5))

    def per_variable(var_slice):
        return cross_pair(var_slice, var_slice)
    result_all = lax.map(per_variable, jnp.moveaxis(spectra, 3, 0)[:, :, :, :, None])
    return jnp.moveaxis(result_all[:, :, 0], 0, 1)
```

```python
import math

import jax
import jax.numpy as jnp
import numpy as np
from jax import lax
from jax.experimental import pallas as pl
from jax.experimental.pallas import tpu as pltpu
from jax.sharding import Mesh, PartitionSpec as P

LON, LAT, MK, NL = 1440, 704, 448, 384
NV, NS, NLEV = 3, 8, 16
NZ, NH, NX, NY, NC = 8, 2, 4, 4, 2
STRIPS = NX * NH * NY
LATL = LAT // STRIPS
LATP = 24
KL = MK // STRIPS
VS = NV * NS
F32, BF16 = jnp.float32, jnp.bfloat16
X0 = 32
X1 = LON // X0


def zonal_factors():
    wave = np.zeros((NC, NX, NY, 32), np.int64)
    part = np.zeros((NC, NX, NY, 32), np.int64)
    live = np.zeros((NC, NX, NY, 32), np.float64)
    for c in range(NC):
        for x in range(NX):
            for y in range(NY):
                for h in range(NH):
                    for zl in range(7):
                        for u in range(2):
                            col = (h * 7 + zl) * 2 + u
                            wave[c, x, y, col] = KL * (x * 8 + h * 4 + y) + 2 * zl + c
                            part[c, x, y, col] = u
                            live[c, x, y, col] = 1.0
    wave, part, live = wave.reshape(-1), part.reshape(-1), live.reshape(-1)
    step = 2.0 * math.pi / LON
    a = step * ((np.arange(X1)[:, None] * X0 * wave[None]) % LON)
    b = step * ((np.arange(X0)[:, None] * wave[None]) % LON)
    scale = live / math.sqrt(LON)
    p = np.where(part == 0, np.cos(a), -np.sin(a)) * scale
    q = np.where(part == 0, -np.sin(a), -np.cos(a)) * scale
    return [t.astype(np.float32) for t in (p, q, np.cos(b), np.sin(b))]


def merid_factors():
    col = np.arange(2 * NL)
    jt, t, jj = col // 256, (col // 128) % 2, col % 128
    m = jt * 128 + jj - NL // 2
    strips = np.array([x * 8 + h * 4 + y for h in range(NH) for x in range(NX) for y in range(NY)])
    step = 2.0 * math.pi / LAT
    a = step * ((strips[:, None] * LATL * m[None]) % LAT)
    b = step * ((np.arange(LATP)[:, None] * m[None]) % LAT)
    keep = (np.arange(LATP) < LATL).astype(np.float64)[:, None]
    p = np.where(t == 0, np.cos(a), np.sin(a)) / math.sqrt(LAT)
    q = np.where(t == 0, -np.sin(a), np.cos(a)) / math.sqrt(LAT)
    return [v.astype(np.float32) for v in (p, q, np.cos(b) * keep, np.sin(b) * keep)]


ROWS = LATL * VS


def zonal_kernel(fl_hbm, fs_hbm, p_ref, q_ref, cb_ref, sb_ref, out_ref, fl, fs, xs, tab, zs, sem):
    cp1 = pltpu.make_async_copy(fl_hbm, fl, sem.at[0])
    cp2 = pltpu.make_async_copy(fs_hbm, fs, sem.at[1])
    cp1.start()
    cp2.start()

    def gen(i, carry):
        row = p_ref[pl.ds(i, 1), :] * cb_ref[...] + q_ref[pl.ds(i, 1), :] * sb_ref[...]
        tab[pl.ds(pl.multiple_of(i * X0, X0), X0), :] = row.astype(BF16)
        return carry

    lax.fori_loop(0, X1, gen, 0)
    zs[:, ROWS:, :] = jnp.zeros((8, VS * LATP - ROWS, 128), F32)
    cp1.wait()
    cp2.wait()

    def diff(i, carry):
        g = pl.ds(i * 6, 6)
        d = fl[g].astype(F32) - fs[g].astype(F32)
        xs[pl.ds(pl.multiple_of(i * 48, 48), 48), :] = d.reshape(48, LON).astype(BF16)
        return carry

    lax.fori_loop(0, 11, diff, 0)
    for n in range(4):
        w = tab[:, n * 256 : (n + 1) * 256]

        def mm(i, carry):
            r = pl.ds(pl.multiple_of(i * 176, 16), 176)
            z = jnp.dot(xs[r, :], w, preferred_element_type=F32)
            zs[2 * n, r, :] = z[:, :128]
            zs[2 * n + 1, r, :] = z[:, 128:]
            return carry

        lax.fori_loop(0, 3, mm, 0)

    lane = lax.broadcasted_iota(jnp.int32, (LATP, 128), 1)
    hi = lane >= 64
    odd = (lane // 32) % 2 == 1

    def move(d, carry):
        for g in range(6):
            a = [zs[d, pl.ds(4 * g + i, LATP, stride=VS), :] for i in range(4)]
            b = [None] * 4
            for i in range(2):
                b[i] = jnp.where(hi, pltpu.roll(a[i + 2], 64, 1), a[i])
                b[i + 2] = jnp.where(hi, a[i + 2], pltpu.roll(a[i], 64, 1))
            o = [None] * 4
            for j in (0, 2):
                o[j] = jnp.where(odd, pltpu.roll(b[j + 1], 32, 1), b[j])
                o[j + 1] = jnp.where(odd, b[j + 1], pltpu.roll(b[j], 96, 1))
            for j in range(4):
                out_ref[4 * d + j, :, 128 * g : 128 * (g + 1)] = o[j].astype(BF16)
        return carry

    lax.fori_loop(0, 8, move, 0)


def zonal(fl, fs):
    vm = pl.BlockSpec(memory_space=pltpu.VMEM)
    return pl.pallas_call(
        zonal_kernel,
        out_shape=jax.ShapeDtypeStruct((32, LATP, 768), BF16),
        in_specs=[pl.BlockSpec(memory_space=pl.ANY)] * 2 + [vm] * 4,
        out_specs=vm,
        scratch_shapes=[
            pltpu.VMEM((66, 8, LON), BF16),
            pltpu.VMEM((66, 8, LON), BF16),
            pltpu.VMEM((ROWS, LON), BF16),
            pltpu.VMEM((LON, 1024), BF16),
            pltpu.VMEM((8, VS * LATP, 128), F32),
            pltpu.SemaphoreType.DMA((2,)),
        ],
        compiler_params=pltpu.CompilerParams(vmem_limit_bytes=40 << 20),
        name="zonal",
    )(fl, fs, *[jnp.asarray(t) for t in zonal_factors()])


def split_kernel(r_ref, y_ref, w):
    for lev in range(2):

        def turn(g, carry):
            x = r_ref[lev, :, :, pl.ds(pl.multiple_of(g * 128, 128), 128)].astype(F32)
            xt = x.reshape(16 * LATP, 128).T
            for t in range(3):
                w[t, pl.ds(pl.multiple_of(g * 128, 128), 128), :] = xt[:, t * 128 : (t + 1) * 128]
            return carry

        lax.fori_loop(0, 6, turn, 0)

        def pick(kidx, carry):
            slot = (kidx % 7) * 2 + kidx // 7
            for t in range(3):
                rows = [w[t, pl.ds(kidx * 2 + u, VS, stride=32), :] for u in range(2)]
                y_ref[slot, lev * 48 : (lev + 1) * 48, t * 128 : (t + 1) * 128] = jnp.concatenate(rows, 0).astype(BF16)
            return carry

        lax.fori_loop(0, 14, pick, 0)


def split_waves(r):
    vm = pl.BlockSpec(memory_space=pltpu.VMEM)
    return pl.pallas_call(
        split_kernel,
        out_shape=jax.ShapeDtypeStruct((16, 96, 384), BF16),
        in_specs=[vm],
        out_specs=vm,
        scratch_shapes=[pltpu.VMEM((3, 768, 128), F32)],
        compiler_params=pltpu.CompilerParams(vmem_limit_bytes=40 << 20),
        name="split_waves",
    )(r)


def pairs_kernel(r_ref, p_ref, q_ref, cb_ref, sb_ref, out_ref, tab, sre, sim):
    for i in range(STRIPS):
        row = p_ref[i : i + 1, :] * cb_ref[...] + q_ref[i : i + 1, :] * sb_ref[...]
        tab[i * LATP : (i + 1) * LATP, :] = row.astype(BF16)

    for jt in range(3):
        cols = slice(jt * 256, (jt + 1) * 256)
        w0 = tab[: 16 * LATP, cols]
        w1 = tab[16 * LATP :, cols]

        def mm(z, carry):
            a0 = r_ref[pl.ds(z * 2, 2), 0].reshape(192, 384)
            a1 = r_ref[pl.ds(z * 2, 2), 1].reshape(192, 384)
            prod = jnp.dot(a0, w0, preferred_element_type=F32) + jnp.dot(a1, w1, preferred_element_type=F32)
            for l in range(4):
                c0 = prod[l * 48 : l * 48 + 24]
                c1 = prod[l * 48 + 24 : l * 48 + 48]
                re = c0[:, :128] + c1[:, 128:]
                im = c1[:, :128] - c0[:, 128:]
                rows = pl.ds(pl.multiple_of(z * 96 + l * 24, 8), 24)
                sre[jt, rows, :] = re.astype(BF16).astype(F32)
                sim[jt, rows, :] = im.astype(BF16).astype(F32)
            return carry

        lax.fori_loop(0, 4, mm, 0)

    def block(n, carry):
        jt = n // NV
        v = n % NV
        bre = [sre[jt, pl.ds(v * NS + s, NLEV, stride=VS), :] for s in range(NS)]
        bim = [sim[jt, pl.ds(v * NS + s, NLEV, stride=VS), :] for s in range(NS)]

        def one(a, inner):
            base = a * VS + v * NS
            co = jnp.zeros((NLEV, 128), F32)
            qd = jnp.zeros((NLEV, 128), F32)
            for s in range(NS):
                ar = sre[jt, pl.ds(base + s, NLEV, stride=0), :]
                ai = sim[jt, pl.ds(base + s, NLEV, stride=0), :]
                co = co + ar * bre[s] + ai * bim[s]
                qd = qd + ai * bre[s] - ar * bim[s]
            lanes = pl.ds(pl.multiple_of(jt * 128, 128), 128)
            out_ref[a, pl.ds(pl.multiple_of(v * 16, 16), 16), lanes] = (co * (1.0 / NS)).astype(BF16)
            out_ref[a, pl.ds(pl.multiple_of(48 + v * 16, 16), 16), lanes] = (qd * (1.0 / NS)).astype(BF16)
            return inner

        lax.fori_loop(0, NLEV, one, 0)
        return carry

    lax.fori_loop(0, 3 * NV, block, 0)


def pairs(r):
    vm = pl.BlockSpec(memory_space=pltpu.VMEM)
    return pl.pallas_call(
        pairs_kernel,
        out_shape=jax.ShapeDtypeStruct((NLEV, 96, NL), BF16),
        in_specs=[vm] * 5,
        out_specs=vm,
        scratch_shapes=[
            pltpu.VMEM((STRIPS * LATP, 2 * NL), BF16),
            pltpu.VMEM((3, NLEV * VS, 128), F32),
            pltpu.VMEM((3, NLEV * VS, 128), F32),
        ],
        compiler_params=pltpu.CompilerParams(vmem_limit_bytes=40 << 20),
        name="pairs",
    )(r, *[jnp.asarray(t) for t in merid_factors()])


def place_kernel(r_ref, out_ref, buf):
    for k in range(KL):
        for t in range(3):
            tile = r_ref[k, :, t * 128 : (t + 1) * 128].astype(F32)
            buf[t, pl.ds(k, 16, stride=16), :] = tile
    for b in range(16):
        for t in range(3):
            out_ref[0, b, :, t * 128 : (t + 1) * 128] = buf[t, b * 16 : b * 16 + KL, :]


def place(r):
    return pl.pallas_call(
        place_kernel,
        grid=(6,),
        out_shape=jax.ShapeDtypeStruct((6, NLEV, KL, NL), F32),
        in_specs=[pl.BlockSpec((16, 16, NL), lambda i: (0, i, 0))],
        out_specs=pl.BlockSpec((1, NLEV, KL, NL), lambda i: (i, 0, 0, 0)),
        scratch_shapes=[pltpu.VMEM((3, 256, 128), F32)],
        compiler_params=pltpu.CompilerParams(vmem_limit_bytes=40 << 20),
        name="place",
    )(r)


def on_device(fc_long, fc_short):
    fl = jnp.transpose(fc_long[:, 0], (0, 2, 1, 3)).reshape(66, NS, LON)
    fs = jnp.transpose(fc_short[:, 0], (0, 2, 1, 3)).reshape(66, NS, LON)
    z = zonal(fl, fs)
    r = lax.all_to_all(z, ("core", "x", "y"), 0, 0, tiled=True)
    y = split_waves(r.reshape(2, 16, LATP, 768))
    r2 = lax.all_to_all(y, ("zl", "zh"), 0, 0, tiled=True)
    c = pairs(r2.reshape(8, 2, 96, 384))
    r3 = lax.all_to_all(c, ("zl", "core"), 0, 0, tiled=True)
    out = place(r3)
    return out.reshape(2, NV, 1, NLEV, KL, NL)


def solution(mesh):
    fine = Mesh(mesh.devices.reshape(NZ, NC, NX, NH, NY), ("zl", "core", "x", "zh", "y"))
    spec = P(("x", "zh", "y"), ("zl", "core"), None, None, None)
    return jax.shard_map(
        on_device,
        mesh=fine,
        in_specs=(spec, spec),
        out_specs=P(None, None, ("zl", "core"), None, ("x", "zh", "y"), None),
        check_vma=False,
    )
```

```python
import math

import jax
import jax.numpy as jnp
import numpy as np
from jax import lax
from jax.experimental import pallas as pl
from jax.experimental.pallas import tpu as pltpu
from jax.sharding import Mesh, PartitionSpec as P

LON, LAT, MK, NL = 1440, 704, 448, 384
NV, NS, NLEV = 3, 8, 16
NZ, NH, NX, NY, NC = 8, 2, 4, 4, 2
STRIPS = NX * NH * NY
LATL = LAT // STRIPS
LATP = 24
KL = MK // STRIPS
VS = NV * NS
F32, BF16 = jnp.float32, jnp.bfloat16
X0 = 32
X1 = LON // X0


def zonal_factors():
    wave = np.zeros((NC, NX, NY, 32), np.int64)
    part = np.zeros((NC, NX, NY, 32), np.int64)
    live = np.zeros((NC, NX, NY, 32), np.float64)
    for c in range(NC):
        for x in range(NX):
            for y in range(NY):
                for h in range(NH):
                    for zl in range(7):
                        for u in range(2):
                            col = (h * 7 + zl) * 2 + u
                            wave[c, x, y, col] = KL * (x * 8 + h * 4 + y) + 2 * zl + c
                            part[c, x, y, col] = u
                            live[c, x, y, col] = 1.0
    wave, part, live = wave.reshape(-1), part.reshape(-1), live.reshape(-1)
    step = 2.0 * math.pi / LON
    a = step * ((np.arange(X1)[:, None] * X0 * wave[None]) % LON)
    b = step * ((np.arange(X0)[:, None] * wave[None]) % LON)
    scale = live / math.sqrt(LON)
    p = np.where(part == 0, np.cos(a), -np.sin(a)) * scale
    q = np.where(part == 0, -np.sin(a), -np.cos(a)) * scale
    return [t.astype(np.float32) for t in (p, q, np.cos(b), np.sin(b))]


def merid_factors():
    col = np.arange(2 * NL)
    jt, t, jj = col // 256, (col // 128) % 2, col % 128
    m = jt * 128 + jj - NL // 2
    strips = np.array([x * 8 + h * 4 + y for h in range(NH) for x in range(NX) for y in range(NY)])
    step = 2.0 * math.pi / LAT
    a = step * ((strips[:, None] * LATL * m[None]) % LAT)
    b = step * ((np.arange(LATP)[:, None] * m[None]) % LAT)
    keep = (np.arange(LATP) < LATL).astype(np.float64)[:, None]
    p = np.where(t == 0, np.cos(a), np.sin(a)) / math.sqrt(LAT)
    q = np.where(t == 0, -np.sin(a), np.cos(a)) / math.sqrt(LAT)
    return [v.astype(np.float32) for v in (p, q, np.cos(b) * keep, np.sin(b) * keep)]


ROWS = LATL * VS


def zonal_kernel(fl_hbm, fs_hbm, f_hbm, out_ref, fl, fs, fac, xs, tab, zs, sem):
    cp0 = pltpu.make_async_copy(f_hbm, fac, sem.at[0])
    cp1 = pltpu.make_async_copy(fl_hbm, fl, sem.at[1])
    cp2 = pltpu.make_async_copy(fs_hbm, fs, sem.at[2])
    cp0.start()
    cp1.start()
    cp2.start()
    zs[:, ROWS:, :] = jnp.zeros((8, VS * LATP - ROWS, 128), F32)
    cp0.wait()

    def gen(i, carry):
        row = fac[pl.ds(i, 1), :] * fac[96:128, :] + fac[pl.ds(48 + i, 1), :] * fac[128:160, :]
        tab[pl.ds(pl.multiple_of(i * X0, X0), X0), :] = row.astype(BF16)
        return carry

    lax.fori_loop(0, X1, gen, 0)
    cp1.wait()
    cp2.wait()

    def diff(i, carry):
        g = pl.ds(i * 6, 6)
        d = fl[g].astype(F32) - fs[g].astype(F32)
        xs[pl.ds(pl.multiple_of(i * 48, 48), 48), :] = d.reshape(48, LON).astype(BF16)
        return carry

    lax.fori_loop(0, 11, diff, 0)

    def mm(n, carry):
        w = tab[:, pl.ds(pl.multiple_of(n * 256, 256), 256)]
        z = jnp.dot(xs[...], w, preferred_element_type=F32)
        zs[2 * n, :ROWS, :] = z[:, :128]
        zs[2 * n + 1, :ROWS, :] = z[:, 128:]
        return carry

    lax.fori_loop(0, 4, mm, 0)

    lane = lax.broadcasted_iota(jnp.int32, (LATP, 128), 1)
    hi = lane >= 64
    odd = (lane // 32) % 2 == 1

    def move(d, carry):
        for g in range(6):
            a = [zs[d, pl.ds(4 * g + i, LATP, stride=VS), :] for i in range(4)]
            b = [None] * 4
            for i in range(2):
                b[i] = jnp.where(hi, pltpu.roll(a[i + 2], 64, 1), a[i])
                b[i + 2] = jnp.where(hi, a[i + 2], pltpu.roll(a[i], 64, 1))
            o = [None] * 4
            for j in (0, 2):
                o[j] = jnp.where(odd, pltpu.roll(b[j + 1], 32, 1), b[j])
                o[j + 1] = jnp.where(odd, b[j + 1], pltpu.roll(b[j], 96, 1))
            for j in range(4):
                out_ref[4 * d + j, :, 128 * g : 128 * (g + 1)] = o[j].astype(BF16)
        return carry

    lax.fori_loop(0, 8, move, 0)


def zonal(fl, fs):
    p, q, cb, sb = zonal_factors()
    fac = np.zeros((160, 1024), np.float32)
    fac[:X1], fac[48 : 48 + X1], fac[96:128], fac[128:] = p, q, cb, sb
    hbm = pl.BlockSpec(memory_space=pltpu.HBM)
    return pl.pallas_call(
        zonal_kernel,
        out_shape=jax.ShapeDtypeStruct((32, LATP, 768), BF16),
        in_specs=[hbm] * 3,
        out_specs=pl.BlockSpec(memory_space=pltpu.VMEM),
        scratch_shapes=[
            pltpu.VMEM((66, 8, LON), BF16),
            pltpu.VMEM((66, 8, LON), BF16),
            pltpu.VMEM((160, 1024), F32),
            pltpu.VMEM((ROWS, LON), BF16),
            pltpu.VMEM((LON, 1024), BF16),
            pltpu.VMEM((8, VS * LATP, 128), F32),
            pltpu.SemaphoreType.DMA((3,)),
        ],
        name="zonal",
    )(fl, fs, jnp.asarray(fac))


def split_kernel(r_ref, y_ref, w):
    for lev in range(2):

        def turn(g, carry):
            x = r_ref[lev, :, :, pl.ds(pl.multiple_of(g * 128, 128), 128)].astype(F32)
            xt = x.reshape(16 * LATP, 128).T
            for t in range(3):
                w[t, pl.ds(pl.multiple_of(g * 128, 128), 128), :] = xt[:, t * 128 : (t + 1) * 128]
            return carry

        lax.fori_loop(0, 6, turn, 0)

        def pick(kidx, carry):
            slot = (kidx % 7) * 2 + kidx // 7
            for t in range(3):
                rows = [w[t, pl.ds(kidx * 2 + u, VS, stride=32), :] for u in range(2)]
                y_ref[slot, lev * 48 : (lev + 1) * 48, t * 128 : (t + 1) * 128] = jnp.concatenate(rows, 0).astype(BF16)
            return carry

        lax.fori_loop(0, 14, pick, 0)


def split_waves(r):
    vm = pl.BlockSpec(memory_space=pltpu.VMEM)
    return pl.pallas_call(
        split_kernel,
        out_shape=jax.ShapeDtypeStruct((16, 96, 384), BF16),
        in_specs=[vm],
        out_specs=vm,
        scratch_shapes=[pltpu.VMEM((3, 768, 128), F32)],
        compiler_params=pltpu.CompilerParams(vmem_limit_bytes=40 << 20),
        name="split_waves",
    )(r)


def table_kernel(f_ref, tab):
    for i in range(STRIPS):
        row = f_ref[i : i + 1, :] * f_ref[64:88, :] + f_ref[32 + i : 33 + i, :] * f_ref[88:112, :]
        tab[i * LATP : (i + 1) * LATP, :] = row.astype(BF16)


def merid_table():
    vm = pl.BlockSpec(memory_space=pltpu.VMEM)
    return pl.pallas_call(
        table_kernel,
        out_shape=jax.ShapeDtypeStruct((STRIPS * LATP, 2 * NL), BF16),
        in_specs=[vm],
        out_specs=vm,
        cost_estimate=pl.CostEstimate(flops=3 * 768 * 768, bytes_accessed=1600000, transcendentals=0),
        compiler_params=pltpu.CompilerParams(vmem_limit_bytes=8 << 20),
        name="merid_table",
    )(jnp.asarray(np.concatenate(merid_factors(), 0)))


def pairs_kernel(r_ref, tab, out_ref, sre, sim):
    a0 = r_ref[:, 0].reshape(768, 384)
    a1 = r_ref[:, 1].reshape(768, 384)

    def merid(jt, carry):
        cols = pl.ds(pl.multiple_of(jt * 256, 256), 256)
        prod = jnp.dot(a0, tab[: 16 * LATP, cols], preferred_element_type=F32)
        prod = prod + jnp.dot(a1, tab[16 * LATP :, cols], preferred_element_type=F32)
        for l in range(NLEV):
            c0 = prod[l * 48 : l * 48 + 24]
            c1 = prod[l * 48 + 24 : l * 48 + 48]
            sre[jt, l * 24 : (l + 1) * 24, :] = (c0[:, :128] + c1[:, 128:]).astype(BF16).astype(F32)
            sim[jt, l * 24 : (l + 1) * 24, :] = (c1[:, :128] - c0[:, 128:]).astype(BF16).astype(F32)
        return carry

    lax.fori_loop(0, 3, merid, 0)

    def block(n, carry):
        jt = n // NV
        v = n % NV
        bre = [sre[jt, pl.ds(v * NS + s, NLEV, stride=VS), :] for s in range(NS)]
        bim = [sim[jt, pl.ds(v * NS + s, NLEV, stride=VS), :] for s in range(NS)]

        def one(a, inner):
            base = a * VS + v * NS
            co = jnp.zeros((NLEV, 128), F32)
            qd = jnp.zeros((NLEV, 128), F32)
            for s in range(NS):
                ar = sre[jt, pl.ds(base + s, NLEV, stride=0), :]
                ai = sim[jt, pl.ds(base + s, NLEV, stride=0), :]
                co = co + ar * bre[s] + ai * bim[s]
                qd = qd + ai * bre[s] - ar * bim[s]
            lanes = pl.ds(pl.multiple_of(jt * 128, 128), 128)
            out_ref[a, pl.ds(pl.multiple_of(v * 16, 16), 16), lanes] = (co * (1.0 / NS)).astype(BF16)
            out_ref[a, pl.ds(pl.multiple_of(48 + v * 16, 16), 16), lanes] = (qd * (1.0 / NS)).astype(BF16)
            return inner

        lax.fori_loop(0, NLEV, one, 0)
        return carry

    lax.fori_loop(0, 3 * NV, block, 0)


def pairs(r, tab):
    vm = pl.BlockSpec(memory_space=pltpu.VMEM)
    return pl.pallas_call(
        pairs_kernel,
        out_shape=jax.ShapeDtypeStruct((NLEV, 96, NL), BF16),
        in_specs=[vm] * 2,
        out_specs=vm,
        scratch_shapes=[
            pltpu.VMEM((3, NLEV * VS, 128), F32),
            pltpu.VMEM((3, NLEV * VS, 128), F32),
        ],
        compiler_params=pltpu.CompilerParams(vmem_limit_bytes=40 << 20),
        name="pairs",
    )(r, tab)


def place_kernel(r_ref, out_ref):
    for k in range(KL):
        out_ref[0, k] = r_ref[k].astype(F32)


def place(r):
    return pl.pallas_call(
        place_kernel,
        grid=(6,),
        out_shape=jax.ShapeDtypeStruct((6, KL, NLEV, NL), F32),
        in_specs=[pl.BlockSpec((16, 16, NL), lambda i: (0, i, 0))],
        out_specs=pl.BlockSpec((1, KL, NLEV, NL), lambda i: (i, 0, 0, 0)),
        name="place",
    )(r)


def on_device(fc_long, fc_short):
    fl = jnp.transpose(fc_long[:, 0], (0, 2, 1, 3)).reshape(66, NS, LON)
    fs = jnp.transpose(fc_short[:, 0], (0, 2, 1, 3)).reshape(66, NS, LON)
    z = zonal(fl, fs)
    r = lax.all_to_all(z, ("core", "x", "y"), 0, 0, tiled=True)
    y = split_waves(r.reshape(2, 16, LATP, 768))
    r2 = lax.all_to_all(y, ("zl", "zh"), 0, 0, tiled=True)
    c = pairs(r2.reshape(8, 2, 96, 384), merid_table())
    r3 = lax.all_to_all(c, ("zl", "core"), 0, 0, tiled=True)
    out = place(r3)
    out = out.reshape(2, NV, 1, KL, NLEV, NL)
    return jnp.swapaxes(out, 3, 4)


def solution(mesh):
    fine = Mesh(mesh.devices.reshape(NZ, NC, NX, NH, NY), ("zl", "core", "x", "zh", "y"))
    spec = P(("x", "zh", "y"), ("zl", "core"), None, None, None)
    return jax.shard_map(
        on_device,
        mesh=fine,
        in_specs=(spec, spec),
        out_specs=P(None, None, ("zl", "core"), None, ("x", "zh", "y"), None),
        check_vma=False,
    )
```

```python
import math

import jax
import jax.numpy as jnp
import numpy as np
from jax import lax
from jax.experimental import pallas as pl
from jax.experimental.pallas import tpu as pltpu
from jax.sharding import Mesh, PartitionSpec as P

LON, LAT, MK, NL = 1440, 704, 448, 384
NV, NS, NLEV = 3, 8, 16
NZ, NH, NX, NY, NC = 8, 2, 4, 4, 2
STRIPS = NX * NH * NY
LATL = LAT // STRIPS
LATP = 24
KL = MK // STRIPS
VS = NV * NS
F32, BF16 = jnp.float32, jnp.bfloat16
X0 = 32
X1 = LON // X0


def zonal_factors():
    wave = np.zeros((NC, NX, NY, 32), np.int64)
    part = np.zeros((NC, NX, NY, 32), np.int64)
    live = np.zeros((NC, NX, NY, 32), np.float64)
    for c in range(NC):
        for x in range(NX):
            for y in range(NY):
                for h in range(NH):
                    for zl in range(7):
                        for u in range(2):
                            col = (h * 7 + zl) * 2 + u
                            wave[c, x, y, col] = KL * (x * 8 + h * 4 + y) + 2 * zl + c
                            part[c, x, y, col] = u
                            live[c, x, y, col] = 1.0
    wave, part, live = wave.reshape(-1), part.reshape(-1), live.reshape(-1)
    step = 2.0 * math.pi / LON
    a = step * ((np.arange(X1)[:, None] * X0 * wave[None]) % LON)
    b = step * ((np.arange(X0)[:, None] * wave[None]) % LON)
    scale = live / math.sqrt(LON)
    p = np.where(part == 0, np.cos(a), -np.sin(a)) * scale
    q = np.where(part == 0, -np.sin(a), -np.cos(a)) * scale
    return [t.astype(np.float32) for t in (p, q, np.cos(b), np.sin(b))]


def merid_table():
    col = np.arange(2 * NL)
    jt, t, jj = col // 256, (col // 128) % 2, col % 128
    m = jt * 128 + jj - NL // 2
    out = np.zeros((NH, 384, 2 * NL), np.float64)
    for h in range(NH):
        strips = np.array([x * 8 + h * 4 + y for x in range(NX) for y in range(NY)])
        lats = (strips[:, None] * LATL + np.arange(LATL)[None]).reshape(-1)
        angle = 2.0 * math.pi / LAT * ((lats[:, None] * m[None]) % LAT)
        out[h, : lats.size] = np.where(t == 0, np.cos(angle), np.sin(angle)) / math.sqrt(LAT)
    return jnp.asarray(out.reshape(NH * 384, 2 * NL).astype(np.float32)).astype(BF16)


ROWS = LATL * VS


def zonal_kernel(fl_hbm, fs_hbm, f_hbm, out_ref, fl, fs, fac, xs, tab, zs, sem):
    cp0 = pltpu.make_async_copy(f_hbm, fac, sem.at[0])
    cp1 = pltpu.make_async_copy(fl_hbm, fl, sem.at[1])
    cp2 = pltpu.make_async_copy(fs_hbm, fs, sem.at[2])
    cp0.start()
    cp1.start()
    cp2.start()
    zs[:, ROWS:, :] = jnp.zeros((8, VS * LATP - ROWS, 128), F32)
    cp0.wait()

    def gen(i, carry):
        row = fac[pl.ds(i, 1), :] * fac[96:128, :] + fac[pl.ds(48 + i, 1), :] * fac[128:160, :]
        tab[pl.ds(pl.multiple_of(i * X0, X0), X0), :] = row.astype(BF16)
        return carry

    lax.fori_loop(0, X1, gen, 0)
    cp1.wait()
    cp2.wait()

    def diff(i, carry):
        g = pl.ds(i * 6, 6)
        d = fl[g].astype(F32) - fs[g].astype(F32)
        xs[pl.ds(pl.multiple_of(i * 48, 48), 48), :] = d.reshape(48, LON).astype(BF16)
        return carry

    lax.fori_loop(0, 11, diff, 0)

    def mm(n, carry):
        w = tab[:, pl.ds(pl.multiple_of(n * 256, 256), 256)]
        z = jnp.dot(xs[...], w, preferred_element_type=F32)
        zs[2 * n, :ROWS, :] = z[:, :128]
        zs[2 * n + 1, :ROWS, :] = z[:, 128:]
        return carry

    lax.fori_loop(0, 4, mm, 0)

    lane = lax.broadcasted_iota(jnp.int32, (LATP, 128), 1)
    hi = lane >= 64
    odd = (lane // 32) % 2 == 1

    def move(d, carry):
        for g in range(6):
            a = [zs[d, pl.ds(4 * g + i, LATP, stride=VS), :] for i in range(4)]
            b = [None] * 4
            for i in range(2):
                b[i] = jnp.where(hi, pltpu.roll(a[i + 2], 64, 1), a[i])
                b[i + 2] = jnp.where(hi, a[i + 2], pltpu.roll(a[i], 64, 1))
            o = [None] * 4
            for j in (0, 2):
                o[j] = jnp.where(odd, pltpu.roll(b[j + 1], 32, 1), b[j])
                o[j + 1] = jnp.where(odd, b[j + 1], pltpu.roll(b[j], 96, 1))
            for j in range(4):
                out_ref[4 * d + j, :, 128 * g : 128 * (g + 1)] = o[j].astype(BF16)
        return carry

    lax.fori_loop(0, 8, move, 0)


def zonal(fl, fs):
    p, q, cb, sb = zonal_factors()
    fac = np.zeros((160, 1024), np.float32)
    fac[:X1], fac[48 : 48 + X1], fac[96:128], fac[128:] = p, q, cb, sb
    hbm = pl.BlockSpec(memory_space=pltpu.HBM)
    return pl.pallas_call(
        zonal_kernel,
        out_shape=jax.ShapeDtypeStruct((32, LATP, 768), BF16),
        in_specs=[hbm] * 3,
        out_specs=pl.BlockSpec(memory_space=pltpu.VMEM),
        scratch_shapes=[
            pltpu.VMEM((66, 8, LON), BF16),
            pltpu.VMEM((66, 8, LON), BF16),
            pltpu.VMEM((160, 1024), F32),
            pltpu.VMEM((ROWS, LON), BF16),
            pltpu.VMEM((LON, 1024), BF16),
            pltpu.VMEM((8, VS * LATP, 128), F32),
            pltpu.SemaphoreType.DMA((3,)),
        ],
        name="zonal",
    )(fl, fs, jnp.asarray(fac))


SLOT = 264


def split_kernel(r_ref, y_ref, pack, w):
    for lev in range(2):

        def turn(g, carry):
            lanes = pl.ds(pl.multiple_of(g * 128, 128), 128)
            for i in range(16):
                pack[i * LATL : (i + 1) * LATL, :] = r_ref[lev, i, :LATL, lanes].astype(F32)
            xt = pack[...].T
            rows = pl.ds(pl.multiple_of(g * 128, 128), 128)
            w[lev, 0, rows, :] = xt[:, :128]
            w[lev, 1, rows, :] = xt[:, 128:256]
            w[lev, 2, rows, :] = xt[:, 256:384]
            return carry

        lax.fori_loop(0, 6, turn, 0)
    tail = lax.broadcasted_iota(jnp.int32, (VS, 128), 1) >= 96

    def pick(kidx, carry):
        slot = (kidx % 7) * 2 + kidx // 7
        combos = [(lev, u) for lev in range(2) for u in range(2)]
        for t in range(2):
            rows = [w[lev, t, pl.ds(kidx * 2 + u, VS, stride=32), :] for lev, u in combos]
            y_ref[slot, t * 96 : (t + 1) * 96, :] = jnp.concatenate(rows, 0).astype(BF16)
        rows = [w[lev, 2, pl.ds(kidx * 2 + u, VS, stride=32), :] for lev, u in combos]
        mixed = [jnp.where(tail, pltpu.roll(rows[3], 96 - 32 * c, 1), rows[c]) for c in range(3)]
        y_ref[slot, 192:SLOT, :] = jnp.concatenate(mixed, 0).astype(BF16)
        return carry

    lax.fori_loop(0, 14, pick, 0)
    y_ref[14, :, :] = jnp.zeros((SLOT, 128), BF16)
    y_ref[15, :, :] = jnp.zeros((SLOT, 128), BF16)


def split_waves(r):
    vm = pl.BlockSpec(memory_space=pltpu.VMEM)
    return pl.pallas_call(
        split_kernel,
        out_shape=jax.ShapeDtypeStruct((16, SLOT, 128), BF16),
        in_specs=[vm],
        out_specs=vm,
        scratch_shapes=[pltpu.VMEM((384, 128), F32), pltpu.VMEM((2, 3, 768, 128), F32)],
        compiler_params=pltpu.CompilerParams(vmem_limit_bytes=40 << 20),
        name="split_waves",
    )(r)


def pairs_kernel(r_ref, tab, out_ref, a_ref, sre, sim):
    tail = lax.broadcasted_iota(jnp.int32, (VS, 128), 1)

    def unpack(z, carry):
        rows = pl.ds(pl.multiple_of(z * 96, 32), 96)
        for h in range(NH):
            a_ref[h, rows, 0:128] = r_ref[z, h, 0:96, :]
            a_ref[h, rows, 128:256] = r_ref[z, h, 96:192, :]
            mixed = [r_ref[z, h, 192 + VS * c : 192 + VS * (c + 1), :].astype(F32) for c in range(3)]
            last = pltpu.roll(mixed[0], 32, 1)
            last = jnp.where(tail >= 32, pltpu.roll(mixed[1], 64, 1), last)
            last = jnp.where(tail >= 64, pltpu.roll(mixed[2], 96, 1), last)
            a_ref[h, rows, 256:384] = jnp.concatenate(mixed + [last], 0).astype(BF16)
        return carry

    lax.fori_loop(0, NZ, unpack, 0)
    a0 = a_ref[0]
    a1 = a_ref[1]

    def merid(jt, carry):
        cols = pl.ds(pl.multiple_of(jt * 256, 256), 256)
        prod = jnp.dot(a0, tab[:384, cols], preferred_element_type=F32)
        prod = prod + jnp.dot(a1, tab[384:, cols], preferred_element_type=F32)
        for l in range(NLEV):
            c0 = prod[l * 48 : l * 48 + 24]
            c1 = prod[l * 48 + 24 : l * 48 + 48]
            sre[jt, l * 24 : (l + 1) * 24, :] = (c0[:, :128] + c1[:, 128:]).astype(BF16).astype(F32)
            sim[jt, l * 24 : (l + 1) * 24, :] = (c1[:, :128] - c0[:, 128:]).astype(BF16).astype(F32)
        return carry

    lax.fori_loop(0, 3, merid, 0)

    def block(n, carry):
        jt = n // NV
        v = n % NV
        bre = [sre[jt, pl.ds(v * NS + s, NLEV, stride=VS), :] for s in range(NS)]
        bim = [sim[jt, pl.ds(v * NS + s, NLEV, stride=VS), :] for s in range(NS)]

        def one(a, inner):
            base = a * VS + v * NS
            co = jnp.zeros((NLEV, 128), F32)
            qd = jnp.zeros((NLEV, 128), F32)
            for s in range(NS):
                ar = sre[jt, pl.ds(base + s, NLEV, stride=0), :]
                ai = sim[jt, pl.ds(base + s, NLEV, stride=0), :]
                co = co + ar * bre[s] + ai * bim[s]
                qd = qd + ai * bre[s] - ar * bim[s]
            lanes = pl.ds(pl.multiple_of(jt * 128, 128), 128)
            out_ref[a, pl.ds(pl.multiple_of(v * 16, 16), 16), lanes] = (co * (1.0 / NS)).astype(BF16)
            out_ref[a, pl.ds(pl.multiple_of(48 + v * 16, 16), 16), lanes] = (qd * (1.0 / NS)).astype(BF16)
            return inner

        lax.fori_loop(0, NLEV, one, 0)
        return carry

    lax.fori_loop(0, 3 * NV, block, 0)


def pairs(r, tab):
    vm = pl.BlockSpec(memory_space=pltpu.VMEM)
    return pl.pallas_call(
        pairs_kernel,
        out_shape=jax.ShapeDtypeStruct((NLEV, 96, NL), BF16),
        in_specs=[vm] * 2,
        out_specs=vm,
        scratch_shapes=[
            pltpu.VMEM((NH, 768, 384), BF16),
            pltpu.VMEM((3, NLEV * VS, 128), F32),
            pltpu.VMEM((3, NLEV * VS, 128), F32),
        ],
        compiler_params=pltpu.CompilerParams(vmem_limit_bytes=40 << 20),
        name="pairs",
    )(r, tab)


def place_kernel(r_ref, out_ref):
    for k in range(KL):
        out_ref[0, k] = r_ref[k].astype(F32)


def place(r):
    return pl.pallas_call(
        place_kernel,
        grid=(6,),
        out_shape=jax.ShapeDtypeStruct((6, KL, NLEV, NL), F32),
        in_specs=[pl.BlockSpec((16, 16, NL), lambda i: (0, i, 0))],
        out_specs=pl.BlockSpec((1, KL, NLEV, NL), lambda i: (i, 0, 0, 0)),
        compiler_params=pltpu.CompilerParams(vmem_limit_bytes=16 << 20),
        name="place",
    )(r)


def on_device(fc_long, fc_short):
    fl = jnp.transpose(fc_long[:, 0], (0, 2, 1, 3)).reshape(66, NS, LON)
    fs = jnp.transpose(fc_short[:, 0], (0, 2, 1, 3)).reshape(66, NS, LON)
    z = zonal(fl, fs)
    r = lax.all_to_all(z, ("core", "x", "y"), 0, 0, tiled=True)
    y = split_waves(r.reshape(2, 16, LATP, 768))
    r2 = lax.all_to_all(y, ("zl", "zh"), 0, 0, tiled=True)
    c = pairs(r2.reshape(NZ, NH, SLOT, 128), merid_table())
    r3 = lax.all_to_all(c, ("zl", "core"), 0, 0, tiled=True)
    out = place(r3)
    out = out.reshape(2, NV, 1, KL, NLEV, NL)
    return jnp.swapaxes(out, 3, 4)


def solution(mesh):
    fine = Mesh(mesh.devices.reshape(NZ, NC, NX, NH, NY), ("zl", "core", "x", "zh", "y"))
    spec = P(("x", "zh", "y"), ("zl", "core"), None, None, None)
    return jax.shard_map(
        on_device,
        mesh=fine,
        in_specs=(spec, spec),
        out_specs=P(None, None, ("zl", "core"), None, ("x", "zh", "y"), None),
        check_vma=False,
    )
```

```python
import math

import jax
import jax.numpy as jnp
import numpy as np
from jax import lax
from jax.experimental import pallas as pl
from jax.experimental.pallas import tpu as pltpu
from jax.sharding import Mesh, PartitionSpec as P


LON, LAT, MK, NL = 1440, 704, 448, 384
NV, NS, NLEV = 3, 8, 16
NZ, NH, NX, NY, NC = 8, 2, 4, 4, 2
STRIPS = NX * NH * NY
LATL = LAT // STRIPS
LATP = 24
KL = MK // STRIPS
VS = NV * NS
F32, BF16 = jnp.float32, jnp.bfloat16
X0 = 32
X1 = LON // X0


def zonal_factors():
    wave = np.zeros((NC, NX, NY, 32), np.int64)
    part = np.zeros((NC, NX, NY, 32), np.int64)
    live = np.zeros((NC, NX, NY, 32), np.float64)
    for c in range(NC):
        for x in range(NX):
            for y in range(NY):
                for h in range(NH):
                    for zl in range(7):
                        for u in range(2):
                            col = (h * 7 + zl) * 2 + u
                            wave[c, x, y, col] = KL * (x * 8 + h * 4 + y) + 2 * zl + c
                            part[c, x, y, col] = u
                            live[c, x, y, col] = 1.0
    wave, part, live = wave.reshape(-1), part.reshape(-1), live.reshape(-1)
    step = 2.0 * math.pi / LON
    a = step * ((np.arange(X1)[:, None] * X0 * wave[None]) % LON)
    b = step * ((np.arange(X0)[:, None] * wave[None]) % LON)
    scale = live / math.sqrt(LON)
    p = np.where(part == 0, np.cos(a), -np.sin(a)) * scale
    q = np.where(part == 0, -np.sin(a), -np.cos(a)) * scale
    return [t.astype(np.float32) for t in (p, q, np.cos(b), np.sin(b))]


def merid_table():
    col = np.arange(2 * NL)
    jt, t, jj = col // 256, (col // 128) % 2, col % 128
    m = jt * 128 + jj - NL // 2
    out = np.zeros((NH, 384, 2 * NL), np.float64)
    for h in range(NH):
        strips = np.array([x * 8 + h * 4 + y for x in range(NX) for y in range(NY)])
        lats = (strips[:, None] * LATL + np.arange(LATL)[None]).reshape(-1)
        angle = 2.0 * math.pi / LAT * ((lats[:, None] * m[None]) % LAT)
        out[h, : lats.size] = np.where(t == 0, np.cos(angle), np.sin(angle)) / math.sqrt(LAT)
    return jnp.asarray(out.reshape(NH * 384, 2 * NL).astype(np.float32)).astype(BF16)


ROWS = LATL * VS


def zonal_kernel(fl_hbm, fs_hbm, f_hbm, out_ref, fl, fs, fac, xs, t0, t1, t2, t3, z0, z1, z2, z3, sem):
    tabs, zs = (t0, t1, t2, t3), (z0, z1, z2, z3)
    cp0 = pltpu.make_async_copy(f_hbm, fac, sem.at[0])
    cp1 = pltpu.make_async_copy(fl_hbm, fl, sem.at[1])
    cp2 = pltpu.make_async_copy(fs_hbm, fs, sem.at[2])
    cp0.start()
    cp1.start()
    cp2.start()
    for z in zs:
        z[:, ROWS:, :] = jnp.zeros((2, VS * LATP - ROWS, 128), F32)
    cp0.wait()

    def gen_rows(n, i):
        cols = slice(n * 256, (n + 1) * 256)
        row = fac[pl.ds(i, 1), cols] * fac[96:128, cols] + fac[pl.ds(48 + i, 1), cols] * fac[128:160, cols]
        return row.astype(BF16)

    def gen_first(i, carry):
        for j in range(3):
            t0[pl.ds(pl.multiple_of((i * 3 + j) * X0, X0), X0), :] = gen_rows(0, i * 3 + j)
        return carry

    lax.fori_loop(0, X1 // 3, gen_first, 0)
    cp1.wait()
    cp2.wait()

    def diff(i, carry):
        g = pl.ds(i * 6, 6)
        d = fl[g].astype(F32) - fs[g].astype(F32)
        xs[pl.ds(pl.multiple_of(i * 48, 48), 48), :] = d.reshape(48, LON).astype(BF16)
        return carry

    lax.fori_loop(0, 11, diff, 0)
    lane = lax.broadcasted_iota(jnp.int32, (LATP, 128), 1)
    hi = lane >= 64
    odd = (lane // 32) % 2 == 1

    def move(n, half):
        d = 2 * n + half
        for g in range(6):
            a = [zs[n][half, pl.ds(4 * g + i, LATP, stride=VS), :] for i in range(4)]
            b = [None] * 4
            for i in range(2):
                b[i] = jnp.where(hi, pltpu.roll(a[i + 2], 64, 1), a[i])
                b[i + 2] = jnp.where(hi, a[i + 2], pltpu.roll(a[i], 64, 1))
            o = [None] * 4
            for j in (0, 2):
                o[j] = jnp.where(odd, pltpu.roll(b[j + 1], 32, 1), b[j])
                o[j + 1] = jnp.where(odd, b[j + 1], pltpu.roll(b[j], 96, 1))
            for j in range(4):
                out_ref[4 * d + j, :, 128 * g : 128 * (g + 1)] = o[j].astype(BF16)

    for n in range(4):
        z = jnp.dot(xs[...], tabs[n][...], preferred_element_type=F32)
        if n < 3:
            for i in range(X1):
                tabs[n + 1][i * X0 : (i + 1) * X0, :] = gen_rows(n + 1, i)
        if n:
            move(n - 1, 0)
            move(n - 1, 1)
        zs[n][0, :ROWS, :] = z[:, :128]
        zs[n][1, :ROWS, :] = z[:, 128:]
    move(3, 0)
    move(3, 1)


def zonal(fl, fs):
    p, q, cb, sb = zonal_factors()
    fac = np.zeros((160, 1024), np.float32)
    fac[:X1], fac[48 : 48 + X1], fac[96:128], fac[128:] = p, q, cb, sb
    hbm = pl.BlockSpec(memory_space=pltpu.HBM)
    return pl.pallas_call(
        zonal_kernel,
        out_shape=jax.ShapeDtypeStruct((32, LATP, 768), BF16),
        in_specs=[hbm] * 3,
        out_specs=pl.BlockSpec(memory_space=pltpu.VMEM),
        scratch_shapes=[
            pltpu.VMEM((66, 8, LON), BF16),
            pltpu.VMEM((66, 8, LON), BF16),
            pltpu.VMEM((160, 1024), F32),
            pltpu.VMEM((ROWS, LON), BF16),
        ]
        + [pltpu.VMEM((LON, 256), BF16)] * 4
        + [pltpu.VMEM((2, VS * LATP, 128), F32)] * 4
        + [pltpu.SemaphoreType.DMA((3,))],
        compiler_params=pltpu.CompilerParams(vmem_limit_bytes=65_600_000),
        name="zonal",
    )(fl, fs, jnp.asarray(fac))


SLOT = 264


def split_kernel(r_ref, y_ref, pack, w):
    core = lax.axis_index("core")
    for lev in range(2):

        def turn(g, carry):
            lanes = pl.ds(pl.multiple_of(g * 128, 128), 128)
            for i in range(16):
                pack[i * LATL : (i + 1) * LATL, :] = r_ref[lev, i, :LATL, lanes].astype(F32)
            xt = pack[...].T
            rows = pl.ds(pl.multiple_of(g * 128, 128), 128)
            w[lev, 0, rows, :] = xt[:, :128]
            w[lev, 1, rows, :] = xt[:, 128:256]
            w[lev, 2, rows, :] = xt[:, 256:384]
            return carry

        lax.fori_loop(0, 6, turn, 0)
    tail = lax.broadcasted_iota(jnp.int32, (VS, 128), 1) >= 96

    def pick(kidx, carry):
        slot = (kidx % 7 + core) * 2 + kidx // 7
        combos = [(lev, u) for lev in range(2) for u in range(2)]
        for t in range(2):
            rows = [w[lev, t, pl.ds(kidx * 2 + u, VS, stride=32), :] for lev, u in combos]
            y_ref[slot, t * 96 : (t + 1) * 96, :] = jnp.concatenate(rows, 0).astype(BF16)
        rows = [w[lev, 2, pl.ds(kidx * 2 + u, VS, stride=32), :] for lev, u in combos]
        mixed = [jnp.where(tail, pltpu.roll(rows[3], 96 - 32 * c, 1), rows[c]) for c in range(3)]
        y_ref[slot, 192:SLOT, :] = jnp.concatenate(mixed, 0).astype(BF16)
        return carry

    lax.fori_loop(0, 14, pick, 0)
    for h in range(NH):
        y_ref[14 * (1 - core) + h, :, :] = jnp.zeros((SLOT, 128), BF16)


def split_waves(r):
    vm = pl.BlockSpec(memory_space=pltpu.VMEM)
    return pl.pallas_call(
        split_kernel,
        out_shape=jax.ShapeDtypeStruct((16, SLOT, 128), BF16),
        in_specs=[vm],
        out_specs=vm,
        scratch_shapes=[pltpu.VMEM((384, 128), F32), pltpu.VMEM((2, 3, 768, 128), F32)],
        compiler_params=pltpu.CompilerParams(vmem_limit_bytes=40 << 20),
        name="split_waves",
    )(r)


def products(sre, sim, outs, first):
    zl, core = lax.axis_index("zl"), lax.axis_index("core")

    def block(n, carry):
        jt = n // NV
        v = n % NV
        bre = [sre[jt, pl.ds(v * NS + s, NLEV, stride=VS), :] for s in range(NS)]
        bim = [sim[jt, pl.ds(v * NS + s, NLEV, stride=VS), :] for s in range(NS)]
        lanes = pl.ds(pl.multiple_of(jt * 128, 128), 128)
        for i, out_ref in enumerate(outs):

            def one(half, inner):
                base = ((zl ^ (first + i)) * 2 + (core ^ half)) * VS + v * NS
                co = jnp.zeros((NLEV, 128), F32)
                qd = jnp.zeros((NLEV, 128), F32)
                for s in range(NS):
                    ar = sre[jt, pl.ds(base + s, NLEV, stride=0), :]
                    ai = sim[jt, pl.ds(base + s, NLEV, stride=0), :]
                    co = co + ar * bre[s] + ai * bim[s]
                    qd = qd + ai * bre[s] - ar * bim[s]
                out_ref[half, pl.ds(pl.multiple_of(v * 16, 16), 16), lanes] = (co * (1.0 / NS)).astype(BF16)
                out_ref[half, pl.ds(pl.multiple_of(48 + v * 16, 16), 16), lanes] = (qd * (1.0 / NS)).astype(BF16)
                return inner

            lax.fori_loop(0, 2, one, 0)
        return carry

    lax.fori_loop(0, 3 * NV, block, 0)


def far_kernel(r_ref, tab, sre, sim, o4, o5, o6, o7, a_ref):
    tail = lax.broadcasted_iota(jnp.int32, (VS, 128), 1)

    def unpack(z, carry):
        rows = pl.ds(pl.multiple_of(z * 96, 32), 96)
        for h in range(NH):
            a_ref[h, rows, 0:128] = r_ref[z, h, 0:96, :]
            a_ref[h, rows, 128:256] = r_ref[z, h, 96:192, :]
            mixed = [r_ref[z, h, 192 + VS * c : 192 + VS * (c + 1), :].astype(F32) for c in range(3)]
            last = pltpu.roll(mixed[0], 32, 1)
            last = jnp.where(tail >= 32, pltpu.roll(mixed[1], 64, 1), last)
            last = jnp.where(tail >= 64, pltpu.roll(mixed[2], 96, 1), last)
            a_ref[h, rows, 256:384] = jnp.concatenate(mixed + [last], 0).astype(BF16)
        return carry

    lax.fori_loop(0, NZ, unpack, 0)
    a0 = a_ref[0]
    a1 = a_ref[1]

    def merid(jt, carry):
        cols = pl.ds(pl.multiple_of(jt * 256, 256), 256)
        prod = jnp.dot(a0, tab[:384, cols], preferred_element_type=F32)
        prod = prod + jnp.dot(a1, tab[384:, cols], preferred_element_type=F32)
        for l in range(NLEV):
            c0 = prod[l * 48 : l * 48 + 24]
            c1 = prod[l * 48 + 24 : l * 48 + 48]
            sre[jt, l * 24 : (l + 1) * 24, :] = (c0[:, :128] + c1[:, 128:]).astype(BF16).astype(F32)
            sim[jt, l * 24 : (l + 1) * 24, :] = (c1[:, :128] - c0[:, 128:]).astype(BF16).astype(F32)
        return carry

    lax.fori_loop(0, 3, merid, 0)

    products(sre, sim, (o4, o5, o6, o7), 4)


def near_kernel(sre, sim, o0, o1, o2, o3):
    products(sre, sim, (o0, o1, o2, o3), 0)


ROWSET = jax.ShapeDtypeStruct((2, 96, NL), BF16)
SPEC = jax.ShapeDtypeStruct((3, NLEV * VS, 128), F32)


def far_pairs(r, tab):
    vm = pl.BlockSpec(memory_space=pltpu.VMEM)
    return pl.pallas_call(
        far_kernel,
        out_shape=[SPEC] * 2 + [ROWSET] * 4,
        in_specs=[vm, vm],
        out_specs=[vm] * 6,
        scratch_shapes=[pltpu.VMEM((NH, 768, 384), BF16)],
        compiler_params=pltpu.CompilerParams(vmem_limit_bytes=24 << 20),
        name="far_pairs",
    )(r, tab)


def near_pairs(sre, sim):
    vm = pl.BlockSpec(memory_space=pltpu.VMEM)
    return pl.pallas_call(
        near_kernel,
        out_shape=[ROWSET] * 4,
        in_specs=[vm, vm],
        out_specs=[vm] * 4,
        cost_estimate=pl.CostEstimate(flops=3_000_000_000, bytes_accessed=1_800_000, transcendentals=0),
        compiler_params=pltpu.CompilerParams(vmem_limit_bytes=16 << 20),
        name="near_pairs",
    )(sre, sim)


def place_kernel(chips, keep, *refs):
    n = 2 * len(chips)
    blocks, out, bufs, sem = refs[:n], refs[n + keep], refs[n + keep + 1], refs[n + keep + 2]
    zl, core = lax.axis_index("zl"), lax.axis_index("core")
    source = [((zl ^ d) - (core ^ half), core ^ half) for half in range(2) for d in chips]

    def copy(i):
        step, parity = source[i]
        return pltpu.make_async_copy(bufs.at[i], out.at[:, 2 * step + parity], sem.at[i])

    for i in range(n):

        @pl.when((source[i][0] >= 0) & (source[i][0] <= 6))
        def _():
            for cv in range(6):
                bufs[i, cv] = blocks[i][0, cv * 16 : (cv + 1) * 16, :].astype(F32)
            copy(i).start()

    for i in range(n):

        @pl.when((source[i][0] >= 0) & (source[i][0] <= 6))
        def _():
            copy(i).wait()


def place(chips, blocks, out=None):
    n, keep = len(blocks), int(out is not None)
    specs = [pl.BlockSpec((1, 96, NL), lambda i, j=j: (j, 0, 0)) for _, j in blocks]
    return pl.pallas_call(
        lambda *refs: place_kernel(chips, keep, *refs),
        grid=(1,),
        out_shape=jax.ShapeDtypeStruct((6, KL, NLEV, NL), F32),
        in_specs=specs + [pl.BlockSpec(memory_space=pl.ANY)] * keep,
        out_specs=pl.BlockSpec(memory_space=pl.ANY),
        scratch_shapes=[pltpu.VMEM((n, 6, NLEV, NL), F32), pltpu.SemaphoreType.DMA((n,))],
        input_output_aliases={n: 0} if keep else {},
        cost_estimate=pl.CostEstimate(flops=1_000_000, bytes_accessed=220_000 * n, transcendentals=0),
        compiler_params=pltpu.CompilerParams(vmem_limit_bytes=24 << 20),
        name="place_rest" if keep else "place_first",
    )(*[a for a, _ in blocks], *([out] if keep else []))


def toward(block, d):
    route = [(z * NC + c, (z ^ d) * NC + c) for z in range(NZ) for c in range(NC) if 0 <= z - c <= 6]
    return lax.ppermute(block, ("zl", "core"), route)


def swap_cores(blocks):
    return lax.ppermute(jnp.stack(blocks), "core", [(0, 1), (1, 0)])


def on_device(fc_long, fc_short):
    fl = jnp.transpose(fc_long[:, 0], (0, 2, 1, 3)).reshape(66, NS, LON)
    fs = jnp.transpose(fc_short[:, 0], (0, 2, 1, 3)).reshape(66, NS, LON)
    z = zonal(fl, fs)
    r = lax.all_to_all(z, ("core", "x", "y"), 0, 0, tiled=True)
    y = split_waves(r.reshape(2, 16, LATP, 768))
    r2 = lax.all_to_all(y, ("zl", "zh"), 0, 0, tiled=True)
    sre, sim, *far = far_pairs(r2.reshape(NZ, NH, SLOT, 128), merid_table())
    got = {}
    for d in (4, 5, 6, 7):
        got[d] = toward(far[d - 4], d)
    near = near_pairs(sre, sim)
    got[0] = near[0]
    for d in (3, 2, 1):
        got[d] = toward(near[d], d)
    early, late = (0, 1, 2, 3, 4, 5), (6, 7)
    out = None
    for group in (early, late):
        swapped = swap_cores([got[d][1] for d in group])
        blocks = [(got[d], 0) for d in group] + [(swapped, i) for i in range(len(group))]
        out = place(group, blocks, out)
    out = out.reshape(2, NV, 1, KL, NLEV, NL)
    return jnp.swapaxes(out, 3, 4)


def solution(mesh):
    fine = Mesh(mesh.devices.reshape(NZ, NC, NX, NH, NY), ("zl", "core", "x", "zh", "y"))
    spec = P(("x", "zh", "y"), ("zl", "core"), None, None, None)
    return jax.shard_map(
        on_device,
        mesh=fine,
        in_specs=(spec, spec),
        out_specs=P(None, None, ("zl", "core"), None, ("x", "zh", "y"), None),
        check_vma=False,
    )
```

```python
import math

import jax
import jax.numpy as jnp
import numpy as np
from jax import lax
from jax.experimental import pallas as pl
from jax.experimental.pallas import tpu as pltpu
from jax.sharding import Mesh, PartitionSpec as P


LON, LAT, MK, NL = 1440, 704, 448, 384
NV, NS, NLEV = 3, 8, 16
NZ, NH, NX, NY, NC = 8, 2, 4, 4, 2
STRIPS = NX * NH * NY
LATL = LAT // STRIPS
LATP = 24
KL = MK // STRIPS
VS = NV * NS
F32, BF16 = jnp.float32, jnp.bfloat16
X0 = 32
X1 = LON // X0


def zonal_factors():
    wave = np.zeros((NC, NX, NY, 32), np.int64)
    part = np.zeros((NC, NX, NY, 32), np.int64)
    live = np.zeros((NC, NX, NY, 32), np.float64)
    for c in range(NC):
        for x in range(NX):
            for y in range(NY):
                for h in range(NH):
                    for zl in range(7):
                        for u in range(2):
                            col = (h * 7 + zl) * 2 + u
                            wave[c, x, y, col] = KL * (x * 8 + h * 4 + y) + 2 * zl + c
                            part[c, x, y, col] = u
                            live[c, x, y, col] = 1.0
    wave, part, live = wave.reshape(-1), part.reshape(-1), live.reshape(-1)
    step = 2.0 * math.pi / LON
    a = step * ((np.arange(X1)[:, None] * X0 * wave[None]) % LON)
    b = step * ((np.arange(X0)[:, None] * wave[None]) % LON)
    scale = live / math.sqrt(LON)
    p = np.where(part == 0, np.cos(a), -np.sin(a)) * scale
    q = np.where(part == 0, -np.sin(a), -np.cos(a)) * scale
    return [t.astype(np.float32) for t in (p, q, np.cos(b), np.sin(b))]


def merid_table():
    col = np.arange(2 * NL)
    jt, t, jj = col // 256, (col // 128) % 2, col % 128
    m = jt * 128 + jj - NL // 2
    out = np.zeros((NH, 384, 2 * NL), np.float64)
    for h in range(NH):
        strips = np.array([x * 8 + h * 4 + y for x in range(NX) for y in range(NY)])
        lats = (strips[:, None] * LATL + np.arange(LATL)[None]).reshape(-1)
        angle = 2.0 * math.pi / LAT * ((lats[:, None] * m[None]) % LAT)
        out[h, : lats.size] = np.where(t == 0, np.cos(angle), np.sin(angle)) / math.sqrt(LAT)
    return jnp.asarray(out.reshape(NH * 384, 2 * NL).astype(np.float32)).astype(BF16)


ROWS = LATL * VS


def zonal_kernel(fl_hbm, fs_hbm, f_hbm, out_ref, fl, fs, fac, xs, t0, t1, t2, t3, z0, z1, z2, z3, sem):
    tabs, zs = (t0, t1, t2, t3), (z0, z1, z2, z3)
    cp0 = pltpu.make_async_copy(f_hbm, fac, sem.at[0])
    cp1 = pltpu.make_async_copy(fl_hbm, fl, sem.at[1])
    cp2 = pltpu.make_async_copy(fs_hbm, fs, sem.at[2])
    cp0.start()
    cp1.start()
    cp2.start()
    for z in zs:
        z[:, ROWS:, :] = jnp.zeros((2, VS * LATP - ROWS, 128), F32)
    cp0.wait()

    def gen_rows(n, i):
        cols = slice(n * 256, (n + 1) * 256)
        row = fac[pl.ds(i, 1), cols] * fac[96:128, cols] + fac[pl.ds(48 + i, 1), cols] * fac[128:160, cols]
        return row.astype(BF16)

    def gen_first(i, carry):
        for j in range(3):
            t0[pl.ds(pl.multiple_of((i * 3 + j) * X0, X0), X0), :] = gen_rows(0, i * 3 + j)
        return carry

    lax.fori_loop(0, X1 // 3, gen_first, 0)
    cp1.wait()
    cp2.wait()

    def diff(i, carry):
        g = pl.ds(i * 6, 6)
        d = fl[g].astype(F32) - fs[g].astype(F32)
        xs[pl.ds(pl.multiple_of(i * 48, 48), 48), :] = d.reshape(48, LON).astype(BF16)
        return carry

    lax.fori_loop(0, 11, diff, 0)
    lane = lax.broadcasted_iota(jnp.int32, (LATP, 128), 1)
    hi = lane >= 64
    odd = (lane // 32) % 2 == 1

    def move(n, half):
        d = 2 * n + half
        for g in range(6):
            a = [zs[n][half, pl.ds(4 * g + i, LATP, stride=VS), :] for i in range(4)]
            b = [None] * 4
            for i in range(2):
                b[i] = jnp.where(hi, pltpu.roll(a[i + 2], 64, 1), a[i])
                b[i + 2] = jnp.where(hi, a[i + 2], pltpu.roll(a[i], 64, 1))
            o = [None] * 4
            for j in (0, 2):
                o[j] = jnp.where(odd, pltpu.roll(b[j + 1], 32, 1), b[j])
                o[j + 1] = jnp.where(odd, b[j + 1], pltpu.roll(b[j], 96, 1))
            for j in range(4):
                out_ref[4 * d + j, :, 128 * g : 128 * (g + 1)] = o[j].astype(BF16)

    for n in range(4):
        z = jnp.dot(xs[...], tabs[n][...], preferred_element_type=F32)
        if n < 3:
            for i in range(X1):
                tabs[n + 1][i * X0 : (i + 1) * X0, :] = gen_rows(n + 1, i)
        if n:
            move(n - 1, 0)
            move(n - 1, 1)
        zs[n][0, :ROWS, :] = z[:, :128]
        zs[n][1, :ROWS, :] = z[:, 128:]
    move(3, 0)
    move(3, 1)


def zonal(fl, fs):
    p, q, cb, sb = zonal_factors()
    fac = np.zeros((160, 1024), np.float32)
    fac[:X1], fac[48 : 48 + X1], fac[96:128], fac[128:] = p, q, cb, sb
    hbm = pl.BlockSpec(memory_space=pltpu.HBM)
    return pl.pallas_call(
        zonal_kernel,
        out_shape=jax.ShapeDtypeStruct((32, LATP, 768), BF16),
        in_specs=[hbm] * 3,
        out_specs=pl.BlockSpec(memory_space=pltpu.VMEM),
        scratch_shapes=[
            pltpu.VMEM((66, 8, LON), BF16),
            pltpu.VMEM((66, 8, LON), BF16),
            pltpu.VMEM((160, 1024), F32),
            pltpu.VMEM((ROWS, LON), BF16),
        ]
        + [pltpu.VMEM((LON, 256), BF16)] * 4
        + [pltpu.VMEM((2, VS * LATP, 128), F32)] * 4
        + [pltpu.SemaphoreType.DMA((3,))],
        compiler_params=pltpu.CompilerParams(vmem_limit_bytes=65_600_000),
        name="zonal",
    )(fl, fs, jnp.asarray(fac))


SLOT = 264


def split_kernel(r_ref, y_ref, pack, w):
    core = lax.axis_index("core")
    for lev in range(2):

        def turn(g, carry):
            lanes = pl.ds(pl.multiple_of(g * 128, 128), 128)
            for i in range(16):
                pack[i * LATL : (i + 1) * LATL, :] = r_ref[lev, i, :LATL, lanes].astype(F32)
            xt = pack[...].T
            rows = pl.ds(pl.multiple_of(g * 128, 128), 128)
            w[lev, 0, rows, :] = xt[:, :128]
            w[lev, 1, rows, :] = xt[:, 128:256]
            w[lev, 2, rows, :] = xt[:, 256:384]
            return carry

        lax.fori_loop(0, 6, turn, 0)
    tail = lax.broadcasted_iota(jnp.int32, (VS, 128), 1) >= 96

    def pick(slot, carry):
        zl, h = slot // 2, slot % 2
        kidx = h * 7 + (zl + 7 - core) % 7
        combos = [(lev, u) for lev in range(2) for u in range(2)]
        for t in range(2):
            rows = [w[lev, t, pl.ds(kidx * 2 + u, VS, stride=32), :] for lev, u in combos]
            y_ref[slot, t * 96 : (t + 1) * 96, :] = jnp.concatenate(rows, 0).astype(BF16)
        rows = [w[lev, 2, pl.ds(kidx * 2 + u, VS, stride=32), :] for lev, u in combos]
        mixed = [jnp.where(tail, pltpu.roll(rows[3], 96 - 32 * c, 1), rows[c]) for c in range(3)]
        y_ref[slot, 192:SLOT, :] = jnp.concatenate(mixed, 0).astype(BF16)
        return carry

    lax.fori_loop(0, 16, pick, 0)


def split_waves(r):
    vm = pl.BlockSpec(memory_space=pltpu.VMEM)
    return pl.pallas_call(
        split_kernel,
        out_shape=jax.ShapeDtypeStruct((16, SLOT, 128), BF16),
        in_specs=[vm],
        out_specs=vm,
        scratch_shapes=[pltpu.VMEM((384, 128), F32), pltpu.VMEM((2, 3, 768, 128), F32)],
        compiler_params=pltpu.CompilerParams(vmem_limit_bytes=40 << 20),
        name="split_waves",
    )(r)


def products(sre, sim, outs, first):
    zl, core = lax.axis_index("zl"), lax.axis_index("core")

    def block(n, carry):
        jt = n // NV
        v = n % NV
        bre = [sre[jt, pl.ds(v * NS + s, NLEV, stride=VS), :] for s in range(NS)]
        bim = [sim[jt, pl.ds(v * NS + s, NLEV, stride=VS), :] for s in range(NS)]
        lanes = pl.ds(pl.multiple_of(jt * 128, 128), 128)
        for i, out_ref in enumerate(outs):
            base = ((zl ^ (first + i // 2)) * 2 + (core ^ (i % 2))) * VS + v * NS
            co = jnp.zeros((NLEV, 128), F32)
            qd = jnp.zeros((NLEV, 128), F32)
            for s in range(NS):
                ar = sre[jt, pl.ds(base + s, NLEV, stride=0), :]
                ai = sim[jt, pl.ds(base + s, NLEV, stride=0), :]
                co = co + ar * bre[s] + ai * bim[s]
                qd = qd + ai * bre[s] - ar * bim[s]
            out_ref[pl.ds(pl.multiple_of(v * 16, 16), 16), lanes] = (co * (1.0 / NS)).astype(BF16)
            out_ref[pl.ds(pl.multiple_of(48 + v * 16, 16), 16), lanes] = (qd * (1.0 / NS)).astype(BF16)
        return carry

    lax.fori_loop(0, 3 * NV, block, 0)


def far_kernel(r_ref, tab, sre, sim, *refs):
    outs, a_ref = refs[:8], refs[8]
    tail = lax.broadcasted_iota(jnp.int32, (VS, 128), 1)

    def unpack(z, carry):
        rows = pl.ds(pl.multiple_of(z * 96, 32), 96)
        for h in range(NH):
            a_ref[h, rows, 0:128] = r_ref[z, h, 0:96, :]
            a_ref[h, rows, 128:256] = r_ref[z, h, 96:192, :]
            mixed = [r_ref[z, h, 192 + VS * c : 192 + VS * (c + 1), :].astype(F32) for c in range(3)]
            last = pltpu.roll(mixed[0], 32, 1)
            last = jnp.where(tail >= 32, pltpu.roll(mixed[1], 64, 1), last)
            last = jnp.where(tail >= 64, pltpu.roll(mixed[2], 96, 1), last)
            a_ref[h, rows, 256:384] = jnp.concatenate(mixed + [last], 0).astype(BF16)
        return carry

    lax.fori_loop(0, NZ, unpack, 0)
    a0 = a_ref[0]
    a1 = a_ref[1]

    def merid(jt, carry):
        cols = pl.ds(pl.multiple_of(jt * 256, 256), 256)
        prod = jnp.dot(a0, tab[:384, cols], preferred_element_type=F32)
        prod = prod + jnp.dot(a1, tab[384:, cols], preferred_element_type=F32)
        for l in range(NLEV):
            c0 = prod[l * 48 : l * 48 + 24]
            c1 = prod[l * 48 + 24 : l * 48 + 48]
            sre[jt, l * 24 : (l + 1) * 24, :] = (c0[:, :128] + c1[:, 128:]).astype(BF16).astype(F32)
            sim[jt, l * 24 : (l + 1) * 24, :] = (c1[:, :128] - c0[:, 128:]).astype(BF16).astype(F32)
        return carry

    lax.fori_loop(0, 3, merid, 0)

    products(sre, sim, outs, 4)


def near_kernel(sre, sim, *outs):
    products(sre, sim, outs, 0)


ROWSET = jax.ShapeDtypeStruct((96, NL), BF16)
SPEC = jax.ShapeDtypeStruct((3, NLEV * VS, 128), F32)


def far_pairs(r, tab):
    vm = pl.BlockSpec(memory_space=pltpu.VMEM)
    return pl.pallas_call(
        far_kernel,
        out_shape=[SPEC] * 2 + [ROWSET] * 8,
        in_specs=[vm, vm],
        out_specs=[vm] * 10,
        scratch_shapes=[pltpu.VMEM((NH, 768, 384), BF16)],
        compiler_params=pltpu.CompilerParams(vmem_limit_bytes=24 << 20),
        name="far_pairs",
    )(r, tab)


def near_pairs(sre, sim):
    vm = pl.BlockSpec(memory_space=pltpu.VMEM)
    return pl.pallas_call(
        near_kernel,
        out_shape=[ROWSET] * 8,
        in_specs=[vm, vm],
        out_specs=[vm] * 8,
        cost_estimate=pl.CostEstimate(flops=3_000_000_000, bytes_accessed=1_800_000, transcendentals=0),
        compiler_params=pltpu.CompilerParams(vmem_limit_bytes=16 << 20),
        name="near_pairs",
    )(sre, sim)


def place_kernel(blocks, keep, *refs):
    n = len(blocks)
    rows, out, bufs, sem = refs[:n], refs[n + keep], refs[n + keep + 1], refs[n + keep + 2]
    zl, core = lax.axis_index("zl"), lax.axis_index("core")

    def when_sent(d):
        return (lambda f: f()) if d < 4 else pl.when(((zl ^ d) >= 1) & ((zl ^ d) <= 6))

    def copy(i):
        d, half = blocks[i]
        parity = core ^ half
        wave = 2 * (((zl ^ d) + 7 - parity) % 7) + parity
        return pltpu.make_async_copy(bufs.at[i], out.at[:, wave], sem.at[i])

    for i in range(n):

        @when_sent(blocks[i][0])
        def _():
            for cv in range(6):
                bufs[i, cv] = rows[i][cv * 16 : (cv + 1) * 16, :].astype(F32)
            copy(i).start()

    for i in range(n):

        @when_sent(blocks[i][0])
        def _():
            copy(i).wait()


def place(blocks, rows, out=None):
    n, keep = len(blocks), int(out is not None)
    return pl.pallas_call(
        lambda *refs: place_kernel(blocks, keep, *refs),
        out_shape=jax.ShapeDtypeStruct((6, KL, NLEV, NL), F32),
        in_specs=[pl.BlockSpec(memory_space=pltpu.VMEM)] * n + [pl.BlockSpec(memory_space=pl.ANY)] * keep,
        out_specs=pl.BlockSpec(memory_space=pl.ANY),
        scratch_shapes=[pltpu.VMEM((n, 6, NLEV, NL), F32), pltpu.SemaphoreType.DMA((n,))],
        input_output_aliases={n: 0} if keep else {},
        cost_estimate=pl.CostEstimate(flops=1_000_000, bytes_accessed=220_000 * n, transcendentals=0),
        compiler_params=pltpu.CompilerParams(vmem_limit_bytes=24 << 20),
        name="place_rest" if keep else "place_first",
    )(*rows, *([out] if keep else []))


def toward(block, d, half):
    route = [(z * NC + c, (z ^ d) * NC + (c ^ half)) for z in range(NZ) for c in range(NC) if d < 4 or 1 <= z <= 6]
    return lax.ppermute(block, ("zl", "core"), route)


SENDS = [(d, half) for d in (4, 5, 3, 6, 2, 7, 1, 0) for half in range(2)][:-2] + [(0, 1)]


def on_device(fc_long, fc_short):
    fl = jnp.transpose(fc_long[:, 0], (0, 2, 1, 3)).reshape(66, NS, LON)
    fs = jnp.transpose(fc_short[:, 0], (0, 2, 1, 3)).reshape(66, NS, LON)
    z = zonal(fl, fs)
    r = lax.all_to_all(z, ("core", "x", "y"), 0, 0, tiled=True)
    y = split_waves(r.reshape(2, 16, LATP, 768))
    r2 = lax.all_to_all(y, ("zl", "zh"), 0, 0, tiled=True)
    sre, sim, *far = far_pairs(r2.reshape(NZ, NH, SLOT, 128), merid_table())
    got = {}
    near = near_pairs(sre, sim)
    mine = [*near, *far]
    for d, half in SENDS:
        got[d, half] = toward(mine[2 * d + half], d, half)
    got[0, 0] = near[0]
    first = [(0, 0)] + SENDS[:6]
    out = place(first, [got[b] for b in first])
    rest = SENDS[6:]
    out = place(rest, [got[b] for b in rest], out)
    out = out.reshape(2, NV, 1, KL, NLEV, NL)
    return jnp.swapaxes(out, 3, 4)


def solution(mesh):
    fine = Mesh(mesh.devices.reshape(NZ, NC, NX, NH, NY), ("zl", "core", "x", "zh", "y"))
    spec = P(("x", "zh", "y"), ("zl", "core"), None, None, None)
    return jax.shard_map(
        on_device,
        mesh=fine,
        in_specs=(spec, spec),
        out_specs=P(None, None, ("zl", "core"), None, ("x", "zh", "y"), None),
        check_vma=False,
    )
```

```python
import math

import jax
import jax.numpy as jnp
import numpy as np
from jax import lax
from jax.experimental import pallas as pl
from jax.experimental.pallas import tpu as pltpu
from jax.sharding import Mesh, PartitionSpec as P


LON, LAT, MK, NL = 1440, 704, 448, 384
NV, NS, NLEV = 3, 8, 16
NZ, NH, NX, NY, NC = 8, 2, 4, 4, 2
STRIPS = NX * NH * NY
LATL = LAT // STRIPS
LATP = 24
KL = MK // STRIPS
VS = NV * NS
F32, BF16 = jnp.float32, jnp.bfloat16
X0 = 32
X1 = LON // X0


def zonal_factors():
    wave = np.zeros((NC, NX, NY, 32), np.int64)
    part = np.zeros((NC, NX, NY, 32), np.int64)
    live = np.zeros((NC, NX, NY, 32), np.float64)
    for c in range(NC):
        for x in range(NX):
            for y in range(NY):
                for h in range(NH):
                    for zl in range(7):
                        for u in range(2):
                            col = (h * 7 + zl) * 2 + u
                            wave[c, x, y, col] = KL * (x * 8 + h * 4 + y) + 2 * zl + c
                            part[c, x, y, col] = u
                            live[c, x, y, col] = 1.0
    wave, part, live = wave.reshape(-1), part.reshape(-1), live.reshape(-1)
    step = 2.0 * math.pi / LON
    a = step * ((np.arange(X1)[:, None] * X0 * wave[None]) % LON)
    b = step * ((np.arange(X0)[:, None] * wave[None]) % LON)
    scale = live / math.sqrt(LON)
    p = np.where(part == 0, np.cos(a), -np.sin(a)) * scale
    q = np.where(part == 0, -np.sin(a), -np.cos(a)) * scale
    return [t.astype(np.float32) for t in (p, q, np.cos(b), np.sin(b))]


def merid_table():
    col = np.arange(2 * NL)
    jt, t, jj = col // 256, (col // 128) % 2, col % 128
    m = jt * 128 + jj - NL // 2
    out = np.zeros((NH, 384, 2 * NL), np.float64)
    for h in range(NH):
        strips = np.array([x * 8 + h * 4 + y for x in range(NX) for y in range(NY)])
        lats = (strips[:, None] * LATL + np.arange(LATL)[None]).reshape(-1)
        angle = 2.0 * math.pi / LAT * ((lats[:, None] * m[None]) % LAT)
        out[h, : lats.size] = np.where(t == 0, np.cos(angle), np.sin(angle)) / math.sqrt(LAT)
    return jnp.asarray(out.reshape(NH * 384, 2 * NL).astype(np.float32)).astype(BF16)


ROWS = LATL * VS


def zonal_kernel(fl_hbm, fs_hbm, f_hbm, out_ref, fl, fs, fac, xs, t0, t1, t2, t3, z0, z1, z2, z3, sem):
    tabs, zs = (t0, t1, t2, t3), (z0, z1, z2, z3)
    cp0 = pltpu.make_async_copy(f_hbm, fac, sem.at[0])
    cp1 = pltpu.make_async_copy(fl_hbm, fl, sem.at[1])
    cp2 = pltpu.make_async_copy(fs_hbm, fs, sem.at[2])
    cp0.start()
    cp1.start()
    cp2.start()
    for z in zs:
        z[:, ROWS:, :] = jnp.zeros((2, VS * LATP - ROWS, 128), F32)
    cp0.wait()

    def gen_rows(n, i):
        cols = slice(n * 256, (n + 1) * 256)
        row = fac[pl.ds(i, 1), cols] * fac[96:128, cols] + fac[pl.ds(48 + i, 1), cols] * fac[128:160, cols]
        return row.astype(BF16)

    def gen_first(i, carry):
        for j in range(3):
            t0[pl.ds(pl.multiple_of((i * 3 + j) * X0, X0), X0), :] = gen_rows(0, i * 3 + j)
        return carry

    lax.fori_loop(0, X1 // 3, gen_first, 0)
    cp1.wait()
    cp2.wait()

    def diff(i, carry):
        g = pl.ds(i * 6, 6)
        d = fl[g].astype(F32) - fs[g].astype(F32)
        xs[pl.ds(pl.multiple_of(i * 48, 48), 48), :] = d.reshape(48, LON).astype(BF16)
        return carry

    lax.fori_loop(0, 11, diff, 0)
    lane = lax.broadcasted_iota(jnp.int32, (LATP, 128), 1)
    hi = lane >= 64
    odd = (lane // 32) % 2 == 1

    def move(n, half):
        d = 2 * n + half
        for g in range(6):
            a = [zs[n][half, pl.ds(4 * g + i, LATP, stride=VS), :] for i in range(4)]
            b = [None] * 4
            for i in range(2):
                b[i] = jnp.where(hi, pltpu.roll(a[i + 2], 64, 1), a[i])
                b[i + 2] = jnp.where(hi, a[i + 2], pltpu.roll(a[i], 64, 1))
            o = [None] * 4
            for j in (0, 2):
                o[j] = jnp.where(odd, pltpu.roll(b[j + 1], 32, 1), b[j])
                o[j + 1] = jnp.where(odd, b[j + 1], pltpu.roll(b[j], 96, 1))
            for j in range(4):
                out_ref[4 * d + j, :, 128 * g : 128 * (g + 1)] = o[j].astype(BF16)

    for n in range(4):
        z = jnp.dot(xs[...], tabs[n][...], preferred_element_type=F32)
        if n < 3:
            for i in range(X1):
                tabs[n + 1][i * X0 : (i + 1) * X0, :] = gen_rows(n + 1, i)
        if n:
            move(n - 1, 0)
            move(n - 1, 1)
        zs[n][0, :ROWS, :] = z[:, :128]
        zs[n][1, :ROWS, :] = z[:, 128:]
    move(3, 0)
    move(3, 1)


def zonal(fl, fs):
    p, q, cb, sb = zonal_factors()
    fac = np.zeros((160, 1024), np.float32)
    fac[:X1], fac[48 : 48 + X1], fac[96:128], fac[128:] = p, q, cb, sb
    hbm = pl.BlockSpec(memory_space=pltpu.HBM)
    return pl.pallas_call(
        zonal_kernel,
        out_shape=jax.ShapeDtypeStruct((32, LATP, 768), BF16),
        in_specs=[hbm] * 3,
        out_specs=pl.BlockSpec(memory_space=pltpu.VMEM),
        scratch_shapes=[
            pltpu.VMEM((66, 8, LON), BF16),
            pltpu.VMEM((66, 8, LON), BF16),
            pltpu.VMEM((160, 1024), F32),
            pltpu.VMEM((ROWS, LON), BF16),
        ]
        + [pltpu.VMEM((LON, 256), BF16)] * 4
        + [pltpu.VMEM((2, VS * LATP, 128), F32)] * 4
        + [pltpu.SemaphoreType.DMA((3,))],
        compiler_params=pltpu.CompilerParams(vmem_limit_bytes=65_600_000),
        name="zonal",
    )(fl, fs, jnp.asarray(fac))


SLOT = 264


def split_kernel(r_ref, y_ref, pack, w):
    core = lax.axis_index("core")
    for lev in range(2):

        def turn(g, carry):
            lanes = pl.ds(pl.multiple_of(g * 128, 128), 128)
            for i in range(16):
                pack[i * LATL : (i + 1) * LATL, :] = r_ref[lev, i, :LATL, lanes].astype(F32)
            xt = pack[...].T
            rows = pl.ds(pl.multiple_of(g * 128, 128), 128)
            w[lev, 0, rows, :] = xt[:, :128]
            w[lev, 1, rows, :] = xt[:, 128:256]
            w[lev, 2, rows, :] = xt[:, 256:384]
            return carry

        lax.fori_loop(0, 6, turn, 0)
    tail = lax.broadcasted_iota(jnp.int32, (VS, 128), 1) >= 96

    def pick(slot, carry):
        zl, h = slot // 2, slot % 2
        kidx = h * 7 + (zl + 7 - core) % 7
        combos = [(lev, u) for lev in range(2) for u in range(2)]
        for t in range(2):
            rows = [w[lev, t, pl.ds(kidx * 2 + u, VS, stride=32), :] for lev, u in combos]
            y_ref[slot, t * 96 : (t + 1) * 96, :] = jnp.concatenate(rows, 0).astype(BF16)
        rows = [w[lev, 2, pl.ds(kidx * 2 + u, VS, stride=32), :] for lev, u in combos]
        mixed = [jnp.where(tail, pltpu.roll(rows[3], 96 - 32 * c, 1), rows[c]) for c in range(3)]
        y_ref[slot, 192:SLOT, :] = jnp.concatenate(mixed, 0).astype(BF16)
        return carry

    lax.fori_loop(0, 16, pick, 0)


def split_waves(r):
    vm = pl.BlockSpec(memory_space=pltpu.VMEM)
    return pl.pallas_call(
        split_kernel,
        out_shape=jax.ShapeDtypeStruct((16, SLOT, 128), BF16),
        in_specs=[vm],
        out_specs=vm,
        scratch_shapes=[pltpu.VMEM((384, 128), F32), pltpu.VMEM((2, 3, 768, 128), F32)],
        compiler_params=pltpu.CompilerParams(vmem_limit_bytes=40 << 20),
        name="split_waves",
    )(r)


def products(sre, sim, outs, first):
    zl, core = lax.axis_index("zl"), lax.axis_index("core")

    def block(n, carry):
        jt = n // NV
        v = n % NV
        bre = [sre[jt, pl.ds(v * NS + s, NLEV, stride=VS), :] for s in range(NS)]
        bim = [sim[jt, pl.ds(v * NS + s, NLEV, stride=VS), :] for s in range(NS)]
        lanes = pl.ds(pl.multiple_of(jt * 128, 128), 128)
        for i, half in [(i, half) for i in range(len(outs)) for half in range(2)]:
            base = ((zl ^ (first + i)) * 2 + (core ^ half)) * VS + v * NS
            co = jnp.zeros((NLEV, 128), F32)
            qd = jnp.zeros((NLEV, 128), F32)
            for s in range(NS):
                ar = sre[jt, pl.ds(base + s, NLEV, stride=0), :]
                ai = sim[jt, pl.ds(base + s, NLEV, stride=0), :]
                co = co + ar * bre[s] + ai * bim[s]
                qd = qd + ai * bre[s] - ar * bim[s]
            outs[i][half, pl.ds(pl.multiple_of(v * 16, 16), 16), lanes] = (co * (1.0 / NS)).astype(BF16)
            outs[i][half, pl.ds(pl.multiple_of(48 + v * 16, 16), 16), lanes] = (qd * (1.0 / NS)).astype(BF16)
        return carry

    lax.fori_loop(0, 3 * NV, block, 0)


def far_kernel(r_ref, tab, sre, sim, *refs):
    outs, a_ref = refs[:4], refs[4]
    tail = lax.broadcasted_iota(jnp.int32, (VS, 128), 1)

    def unpack(z, carry):
        rows = pl.ds(pl.multiple_of(z * 96, 32), 96)
        for h in range(NH):
            a_ref[h, rows, 0:128] = r_ref[z, h, 0:96, :]
            a_ref[h, rows, 128:256] = r_ref[z, h, 96:192, :]
            mixed = [r_ref[z, h, 192 + VS * c : 192 + VS * (c + 1), :].astype(F32) for c in range(3)]
            last = pltpu.roll(mixed[0], 32, 1)
            last = jnp.where(tail >= 32, pltpu.roll(mixed[1], 64, 1), last)
            last = jnp.where(tail >= 64, pltpu.roll(mixed[2], 96, 1), last)
            a_ref[h, rows, 256:384] = jnp.concatenate(mixed + [last], 0).astype(BF16)
        return carry

    lax.fori_loop(0, NZ, unpack, 0)
    a0 = a_ref[0]
    a1 = a_ref[1]

    def merid(jt, carry):
        cols = pl.ds(pl.multiple_of(jt * 256, 256), 256)
        prod = jnp.dot(a0, tab[:384, cols], preferred_element_type=F32)
        prod = prod + jnp.dot(a1, tab[384:, cols], preferred_element_type=F32)
        for l in range(NLEV):
            c0 = prod[l * 48 : l * 48 + 24]
            c1 = prod[l * 48 + 24 : l * 48 + 48]
            sre[jt, l * 24 : (l + 1) * 24, :] = (c0[:, :128] + c1[:, 128:]).astype(BF16).astype(F32)
            sim[jt, l * 24 : (l + 1) * 24, :] = (c1[:, :128] - c0[:, 128:]).astype(BF16).astype(F32)
        return carry

    lax.fori_loop(0, 3, merid, 0)

    products(sre, sim, outs, 4)


def near_kernel(sre, sim, *outs):
    products(sre, sim, outs, 0)


ROWSET = jax.ShapeDtypeStruct((2, 96, NL), BF16)
SPEC = jax.ShapeDtypeStruct((3, NLEV * VS, 128), F32)


def far_pairs(r, tab):
    vm = pl.BlockSpec(memory_space=pltpu.VMEM)
    return pl.pallas_call(
        far_kernel,
        out_shape=[SPEC] * 2 + [ROWSET] * 4,
        in_specs=[vm, vm],
        out_specs=[vm] * 6,
        scratch_shapes=[pltpu.VMEM((NH, 768, 384), BF16)],
        compiler_params=pltpu.CompilerParams(vmem_limit_bytes=24 << 20),
        name="far_pairs",
    )(r, tab)


def near_pairs(sre, sim):
    vm = pl.BlockSpec(memory_space=pltpu.VMEM)
    return pl.pallas_call(
        near_kernel,
        out_shape=[ROWSET] * 4,
        in_specs=[vm, vm],
        out_specs=[vm] * 4,
        cost_estimate=pl.CostEstimate(flops=3_000_000_000, bytes_accessed=1_800_000, transcendentals=0),
        compiler_params=pltpu.CompilerParams(vmem_limit_bytes=16 << 20),
        name="near_pairs",
    )(sre, sim)


def place_kernel(blocks, keep, *refs):
    n = len(blocks)
    rows, out, bufs, sem = refs[:n], refs[n + keep], refs[n + keep + 1], refs[n + keep + 2]
    zl, core = lax.axis_index("zl"), lax.axis_index("core")

    def when_sent(d):
        return (lambda f: f()) if d < 4 else pl.when(((zl ^ d) >= 1) & ((zl ^ d) <= 6))

    def copy(i):
        d, half = blocks[i]
        parity = core ^ half
        wave = 2 * (((zl ^ d) + 7 - parity) % 7) + parity
        return pltpu.make_async_copy(bufs.at[i], out.at[:, wave], sem.at[i])

    for i in range(n):

        @when_sent(blocks[i][0])
        def _():
            for cv in range(6):
                bufs[i, cv] = rows[i][0, cv * 16 : (cv + 1) * 16, :].astype(F32)
            copy(i).start()

    for i in range(n):

        @when_sent(blocks[i][0])
        def _():
            copy(i).wait()


def place(blocks, rows, out=None):
    n, keep = len(blocks), int(out is not None)
    specs = [pl.BlockSpec((1, 96, NL), lambda i, j=j: (j, 0, 0)) for _, j in rows]
    return pl.pallas_call(
        lambda *refs: place_kernel(blocks, keep, *refs),
        out_shape=jax.ShapeDtypeStruct((6, KL, NLEV, NL), F32),
        grid=(1,),
        in_specs=specs + [pl.BlockSpec(memory_space=pl.ANY)] * keep,
        out_specs=pl.BlockSpec(memory_space=pl.ANY),
        scratch_shapes=[pltpu.VMEM((n, 6, NLEV, NL), F32), pltpu.SemaphoreType.DMA((n,))],
        input_output_aliases={n: 0} if keep else {},
        cost_estimate=pl.CostEstimate(flops=1_000_000, bytes_accessed=220_000 * n, transcendentals=0),
        compiler_params=pltpu.CompilerParams(vmem_limit_bytes=24 << 20),
        name="place_rest" if keep else "place_first",
    )(*[a for a, _ in rows], *([out] if keep else []))


def toward(block, d):
    route = [(z * NC + c, (z ^ d) * NC + c) for z in range(NZ) for c in range(NC) if d < 4 or 1 <= z <= 6]
    return lax.ppermute(block, ("zl", "core"), route)


def swap_cores(blocks):
    return lax.ppermute(jnp.stack(blocks), "core", [(0, 1), (1, 0)])


SENDS = (4, 5, 6, 3, 7, 2, 1)
GROUPS = ((0, 4, 5, 3), (6, 7, 2, 1))


def on_device(fc_long, fc_short):
    fl = jnp.transpose(fc_long[:, 0], (0, 2, 1, 3)).reshape(66, NS, LON)
    fs = jnp.transpose(fc_short[:, 0], (0, 2, 1, 3)).reshape(66, NS, LON)
    z = zonal(fl, fs)
    r = lax.all_to_all(z, ("core", "x", "y"), 0, 0, tiled=True)
    y = split_waves(r.reshape(2, 16, LATP, 768))
    r2 = lax.all_to_all(y, ("zl", "zh"), 0, 0, tiled=True)
    sre, sim, *far = far_pairs(r2.reshape(NZ, NH, SLOT, 128), merid_table())
    out = None
    near = near_pairs(sre, sim)
    mine = [*near, *far]
    got = {0: near[0]}
    for d in SENDS:
        got[d] = toward(mine[d], d)
    for group in GROUPS:
        swapped = swap_cores([got[d][1] for d in group])
        rows = [(got[d], 0) for d in group] + [(swapped, i) for i in range(len(group))]
        out = place([(d, half) for half in range(2) for d in group], rows, out)
    out = out.reshape(2, NV, 1, KL, NLEV, NL)
    return jnp.swapaxes(out, 3, 4)


def solution(mesh):
    fine = Mesh(mesh.devices.reshape(NZ, NC, NX, NH, NY), ("zl", "core", "x", "zh", "y"))
    spec = P(("x", "zh", "y"), ("zl", "core"), None, None, None)
    return jax.shard_map(
        on_device,
        mesh=fine,
        in_specs=(spec, spec),
        out_specs=P(None, None, ("zl", "core"), None, ("x", "zh", "y"), None),
        check_vma=False,
    )
```

```python
import math

import jax
import jax.numpy as jnp
import numpy as np
from jax import lax
from jax.experimental import pallas as pl
from jax.experimental.pallas import tpu as pltpu
from jax.sharding import Mesh, PartitionSpec as P


LON, LAT, MK, NL = 1440, 704, 448, 384
NV, NS, NLEV = 3, 8, 16
NZ, NH, NX, NY, NC = 8, 2, 4, 4, 2
STRIPS = NX * NH * NY
LATL = LAT // STRIPS
LATP = 24
KL = MK // STRIPS
VS = NV * NS
F32, BF16 = jnp.float32, jnp.bfloat16
X0 = 32
X1 = LON // X0


def zonal_factors():
    wave = np.zeros((NC, NX, NY, 32), np.int64)
    part = np.zeros((NC, NX, NY, 32), np.int64)
    live = np.zeros((NC, NX, NY, 32), np.float64)
    for c in range(NC):
        for x in range(NX):
            for y in range(NY):
                for h in range(NH):
                    for zl in range(7):
                        for u in range(2):
                            col = (h * 7 + zl) * 2 + u
                            wave[c, x, y, col] = KL * (x * 8 + h * 4 + y) + 2 * zl + c
                            part[c, x, y, col] = u
                            live[c, x, y, col] = 1.0
    wave, part, live = wave.reshape(-1), part.reshape(-1), live.reshape(-1)
    step = 2.0 * math.pi / LON
    a = step * ((np.arange(X1)[:, None] * X0 * wave[None]) % LON)
    b = step * ((np.arange(X0)[:, None] * wave[None]) % LON)
    scale = live / math.sqrt(LON)
    p = np.where(part == 0, np.cos(a), -np.sin(a)) * scale
    q = np.where(part == 0, -np.sin(a), -np.cos(a)) * scale
    return [t.astype(np.float32) for t in (p, q, np.cos(b), np.sin(b))]


def merid_table():
    col = np.arange(2 * NL)
    jt, t, jj = col // 256, (col // 128) % 2, col % 128
    m = jt * 128 + jj - NL // 2
    out = np.zeros((NH, 384, 2 * NL), np.float64)
    for h in range(NH):
        strips = np.array([x * 8 + h * 4 + y for x in range(NX) for y in range(NY)])
        lats = (strips[:, None] * LATL + np.arange(LATL)[None]).reshape(-1)
        angle = 2.0 * math.pi / LAT * ((lats[:, None] * m[None]) % LAT)
        out[h, : lats.size] = np.where(t == 0, np.cos(angle), np.sin(angle)) / math.sqrt(LAT)
    return jnp.asarray(out.reshape(NH * 384, 2 * NL).astype(np.float32)).astype(BF16)


ROWS = LATL * VS


def zonal_kernel(fl_hbm, fs_hbm, f_hbm, out_ref, fl, fs, fac, xs, t0, t1, t2, t3, z0, z1, z2, z3, sem):
    tabs, zs = (t0, t1, t2, t3), (z0, z1, z2, z3)
    cp0 = pltpu.make_async_copy(f_hbm, fac, sem.at[0])
    cp0.start()
    cuts = (0, 24, 66)
    loads = []
    for n in range(2):
        g = pl.ds(cuts[n], cuts[n + 1] - cuts[n])
        pair = [pltpu.make_async_copy(src.at[g], dst.at[g], sem.at[1 + 2 * n + i]) for i, (src, dst) in enumerate(((fl_hbm, fl), (fs_hbm, fs)))]
        for c in pair:
            c.start()
        loads.append(pair)
    for z in zs:
        z[:, ROWS:, :] = jnp.zeros((2, VS * LATP - ROWS, 128), F32)
    cp0.wait()

    def gen_rows(n, i):
        cols = slice(n * 256, (n + 1) * 256)
        row = fac[pl.ds(i, 1), cols] * fac[96:128, cols] + fac[pl.ds(48 + i, 1), cols] * fac[128:160, cols]
        return row.astype(BF16)

    def gen_first(i, carry):
        for j in range(3):
            t0[pl.ds(pl.multiple_of((i * 3 + j) * X0, X0), X0), :] = gen_rows(0, i * 3 + j)
        return carry

    lax.fori_loop(0, X1 // 3, gen_first, 0)

    def diff(i, carry):
        g = pl.ds(i * 6, 6)
        d = fl[g].astype(F32) - fs[g].astype(F32)
        xs[pl.ds(pl.multiple_of(i * 48, 48), 48), :] = d.reshape(48, LON).astype(BF16)
        return carry

    for n in range(2):
        for c in loads[n]:
            c.wait()
        lax.fori_loop(cuts[n] // 6, cuts[n + 1] // 6, diff, 0)
    lane = lax.broadcasted_iota(jnp.int32, (LATP, 128), 1)
    hi = lane >= 64
    odd = (lane // 32) % 2 == 1

    def move(n, half):
        d = 2 * n + half
        for g in range(6):
            a = [zs[n][half, pl.ds(4 * g + i, LATP, stride=VS), :] for i in range(4)]
            b = [None] * 4
            for i in range(2):
                b[i] = jnp.where(hi, pltpu.roll(a[i + 2], 64, 1), a[i])
                b[i + 2] = jnp.where(hi, a[i + 2], pltpu.roll(a[i], 64, 1))
            o = [None] * 4
            for j in (0, 2):
                o[j] = jnp.where(odd, pltpu.roll(b[j + 1], 32, 1), b[j])
                o[j + 1] = jnp.where(odd, b[j + 1], pltpu.roll(b[j], 96, 1))
            for j in range(4):
                out_ref[4 * d + j, :, 128 * g : 128 * (g + 1)] = o[j].astype(BF16)

    for n in range(4):
        z = jnp.dot(xs[...], tabs[n][...], preferred_element_type=F32)
        if n < 3:
            for i in range(X1):
                tabs[n + 1][i * X0 : (i + 1) * X0, :] = gen_rows(n + 1, i)
        if n:
            move(n - 1, 0)
            move(n - 1, 1)
        zs[n][0, :ROWS, :] = z[:, :128]
        zs[n][1, :ROWS, :] = z[:, 128:]
    move(3, 0)
    move(3, 1)


def zonal(fl, fs):
    p, q, cb, sb = zonal_factors()
    fac = np.zeros((160, 1024), np.float32)
    fac[:X1], fac[48 : 48 + X1], fac[96:128], fac[128:] = p, q, cb, sb
    hbm = pl.BlockSpec(memory_space=pltpu.HBM)
    return pl.pallas_call(
        zonal_kernel,
        out_shape=jax.ShapeDtypeStruct((32, LATP, 768), BF16),
        in_specs=[hbm] * 3,
        out_specs=pl.BlockSpec(memory_space=pltpu.VMEM),
        scratch_shapes=[
            pltpu.VMEM((66, 8, LON), BF16),
            pltpu.VMEM((66, 8, LON), BF16),
            pltpu.VMEM((160, 1024), F32),
            pltpu.VMEM((ROWS, LON), BF16),
        ]
        + [pltpu.VMEM((LON, 256), BF16)] * 4
        + [pltpu.VMEM((2, VS * LATP, 128), F32)] * 4
        + [pltpu.SemaphoreType.DMA((5,))],
        compiler_params=pltpu.CompilerParams(vmem_limit_bytes=32 << 20),
        name="zonal",
    )(*[pltpu.with_memory_space_constraint(t, pltpu.HBM) for t in (fl, fs, jnp.asarray(fac))])


SLOT = 264
PITCH = 40


def split_kernel(r_ref, y_ref, pack, w):
    core = lax.axis_index("core")
    for lev in range(2):

        def turn(g, carry):
            lanes = pl.ds(pl.multiple_of(g * 128, 128), 128)
            for i in range(16):
                pack[i * LATL : (i + 1) * LATL, :] = r_ref[lev, i, :LATL, lanes].astype(F32)
            xt = pack[...].T
            for i in range(4):
                rows = pl.ds(pl.multiple_of((g * 4 + i) * PITCH, 8), 32)
                for t in range(3):
                    w[lev, t, rows, :] = xt[32 * i : 32 * (i + 1), 128 * t : 128 * (t + 1)]
            return carry

        lax.fori_loop(0, 6, turn, 0)
    tail = lax.broadcasted_iota(jnp.int32, (VS, 128), 1) >= 96

    def pick(slot, carry):
        zl, h = slot // 2, slot % 2
        kidx = h * 7 + (zl + 7 - core) % 7
        combos = [(lev, u) for lev in range(2) for u in range(2)]
        for t in range(2):
            rows = [w[lev, t, pl.ds(kidx * 2 + u, VS, stride=PITCH), :] for lev, u in combos]
            y_ref[slot, t * 96 : (t + 1) * 96, :] = jnp.concatenate(rows, 0).astype(BF16)
        rows = [w[lev, 2, pl.ds(kidx * 2 + u, VS, stride=PITCH), :] for lev, u in combos]
        mixed = [jnp.where(tail, pltpu.roll(rows[3], 96 - 32 * c, 1), rows[c]) for c in range(3)]
        y_ref[slot, 192:SLOT, :] = jnp.concatenate(mixed, 0).astype(BF16)
        return carry

    lax.fori_loop(0, 16, pick, 0)


def split_waves(r):
    vm = pl.BlockSpec(memory_space=pltpu.VMEM)
    return pl.pallas_call(
        split_kernel,
        out_shape=jax.ShapeDtypeStruct((16, SLOT, 128), BF16),
        in_specs=[vm],
        out_specs=vm,
        scratch_shapes=[pltpu.VMEM((384, 128), F32), pltpu.VMEM((2, 3, VS * PITCH, 128), F32)],
        compiler_params=pltpu.CompilerParams(vmem_limit_bytes=40 << 20),
        name="split_waves",
    )(r)


def products(sre, sim, outs, chips):
    zl, core = lax.axis_index("zl"), lax.axis_index("core")

    def block(n, carry):
        jt = n // NV
        v = n % NV
        bre = [sre[jt, pl.ds(v * NS + s, NLEV, stride=VS), :] for s in range(NS)]
        bim = [sim[jt, pl.ds(v * NS + s, NLEV, stride=VS), :] for s in range(NS)]
        lanes = pl.ds(pl.multiple_of(jt * 128, 128), 128)
        for i, half in [(i, half) for i in range(len(outs)) for half in range(2)]:
            base = ((zl ^ chips[i]) * 2 + (core ^ half)) * VS + v * NS
            co = jnp.zeros((NLEV, 128), F32)
            qd = jnp.zeros((NLEV, 128), F32)
            for s in range(NS):
                ar = sre[jt, pl.ds(base + s, NLEV, stride=0), :]
                ai = sim[jt, pl.ds(base + s, NLEV, stride=0), :]
                co = co + ar * bre[s] + ai * bim[s]
                qd = qd + ai * bre[s] - ar * bim[s]
            outs[i][half, pl.ds(pl.multiple_of(v * 16, 16), 16), lanes] = (co * (1.0 / NS)).astype(BF16)
            outs[i][half, pl.ds(pl.multiple_of(48 + v * 16, 16), 16), lanes] = (qd * (1.0 / NS)).astype(BF16)
        return carry

    lax.fori_loop(0, 3 * NV, block, 0)


def far_kernel(r_ref, tab, sre, sim, *refs):
    outs, a_ref = refs[:2], refs[2]
    tail = lax.broadcasted_iota(jnp.int32, (VS, 128), 1)

    def unpack(z, carry):
        rows = pl.ds(pl.multiple_of(z * 96, 32), 96)
        for h in range(NH):
            at = h * 384
            a_ref[rows, at : at + 128] = r_ref[z, h, 0:96, :]
            a_ref[rows, at + 128 : at + 256] = r_ref[z, h, 96:192, :]
            mixed = [r_ref[z, h, 192 + VS * c : 192 + VS * (c + 1), :].astype(F32) for c in range(3)]
            last = pltpu.roll(mixed[0], 32, 1)
            last = jnp.where(tail >= 32, pltpu.roll(mixed[1], 64, 1), last)
            last = jnp.where(tail >= 64, pltpu.roll(mixed[2], 96, 1), last)
            a_ref[rows, at + 256 : at + 384] = jnp.concatenate(mixed + [last], 0).astype(BF16)
        return carry

    lax.fori_loop(0, NZ, unpack, 0)

    def merid(jt, carry):
        cols = pl.ds(pl.multiple_of(jt * 256, 256), 256)
        prod = jnp.dot(a_ref[...], tab[:, cols], preferred_element_type=F32)
        for l in range(NLEV):
            c0 = prod[l * 48 : l * 48 + 24]
            c1 = prod[l * 48 + 24 : l * 48 + 48]
            sre[jt, l * 24 : (l + 1) * 24, :] = (c0[:, :128] + c1[:, 128:]).astype(BF16).astype(F32)
            sim[jt, l * 24 : (l + 1) * 24, :] = (c1[:, :128] - c0[:, 128:]).astype(BF16).astype(F32)
        return carry

    lax.fori_loop(0, 3, merid, 0)

    products(sre, sim, outs, FIRST)


def near_kernel(sre, sim, *outs):
    products(sre, sim, outs, OTHER)


FIRST, OTHER = (4, 5), (6, 3, 7, 2, 1, 0)
ROWSET = jax.ShapeDtypeStruct((2, 96, NL), BF16)
SPEC = jax.ShapeDtypeStruct((3, NLEV * VS, 128), F32)


def far_pairs(r, tab):
    vm = pl.BlockSpec(memory_space=pltpu.VMEM)
    return pl.pallas_call(
        far_kernel,
        out_shape=[SPEC] * 2 + [ROWSET] * 2,
        in_specs=[vm, vm],
        out_specs=[vm] * 4,
        scratch_shapes=[pltpu.VMEM((768, NH * 384), BF16)],
        compiler_params=pltpu.CompilerParams(vmem_limit_bytes=24 << 20),
        name="far_pairs",
    )(r, tab)


def near_pairs(sre, sim):
    vm = pl.BlockSpec(memory_space=pltpu.VMEM)
    return pl.pallas_call(
        near_kernel,
        out_shape=[ROWSET] * len(OTHER),
        in_specs=[vm, vm],
        out_specs=[vm] * len(OTHER),
        cost_estimate=pl.CostEstimate(flops=3_000_000_000, bytes_accessed=1_800_000, transcendentals=0),
        compiler_params=pltpu.CompilerParams(vmem_limit_bytes=16 << 20),
        name="near_pairs",
    )(sre, sim)


def place_kernel(blocks, keep, *refs):
    n = len(blocks)
    rows, out, bufs, sem = refs[:n], refs[n + keep], refs[n + keep + 1], refs[n + keep + 2]
    zl, core = lax.axis_index("zl"), lax.axis_index("core")

    def when_sent(d):
        return (lambda f: f()) if d < 4 else pl.when(((zl ^ d) >= 1) & ((zl ^ d) <= 6))

    def copy(i):
        d, half = blocks[i]
        parity = core ^ half
        wave = 2 * (((zl ^ d) + 7 - parity) % 7) + parity
        return pltpu.make_async_copy(bufs.at[i], out.at[:, wave], sem.at[i])

    for i in range(n):

        @when_sent(blocks[i][0])
        def _():
            for cv in range(6):
                bufs[i, cv] = rows[i][0, cv * 16 : (cv + 1) * 16, :].astype(F32)
            copy(i).start()

    for i in range(n):

        @when_sent(blocks[i][0])
        def _():
            copy(i).wait()


def place(blocks, rows, out=None):
    n, keep = len(blocks), int(out is not None)
    specs = [pl.BlockSpec((1, 96, NL), lambda i, j=j: (j, 0, 0)) for _, j in rows]
    return pl.pallas_call(
        lambda *refs: place_kernel(blocks, keep, *refs),
        out_shape=jax.ShapeDtypeStruct((6, KL, NLEV, NL), F32),
        grid=(1,),
        in_specs=specs + [pl.BlockSpec(memory_space=pl.ANY)] * keep,
        out_specs=pl.BlockSpec(memory_space=pl.ANY),
        scratch_shapes=[pltpu.VMEM((n, 6, NLEV, NL), F32), pltpu.SemaphoreType.DMA((n,))],
        input_output_aliases={n: 0} if keep else {},
        cost_estimate=pl.CostEstimate(flops=1_000_000, bytes_accessed=220_000 * n, transcendentals=0),
        compiler_params=pltpu.CompilerParams(vmem_limit_bytes=24 << 20),
        name="place_rest" if keep else "place_first",
    )(*[a for a, _ in rows], *([out] if keep else []))


def toward(block, d):
    route = [(z * NC + c, (z ^ d) * NC + c) for z in range(NZ) for c in range(NC) if d < 4 or 1 <= z <= 6]
    return lax.ppermute(block, ("zl", "core"), route)


def swap_cores(blocks):
    return lax.ppermute(jnp.stack(blocks), "core", [(0, 1), (1, 0)])


SENDS = (4, 5, 6, 3, 7, 2, 1)
GROUPS = ((0, 4, 5), (6, 3, 7, 2, 1))


def on_device(fc_long, fc_short):
    fl = jnp.transpose(fc_long[:, 0], (0, 2, 1, 3)).reshape(66, NS, LON)
    fs = jnp.transpose(fc_short[:, 0], (0, 2, 1, 3)).reshape(66, NS, LON)
    z = zonal(fl, fs)
    r = lax.all_to_all(z, ("core", "x", "y"), 0, 0, tiled=True)
    y = split_waves(r.reshape(2, 16, LATP, 768))
    r2 = lax.all_to_all(y, ("zl", "zh"), 0, 0, tiled=True)
    sre, sim, *far = far_pairs(r2.reshape(NZ, NH, SLOT, 128), merid_table())
    out = None
    near = near_pairs(sre, sim)
    mine = dict(zip(FIRST + OTHER, [*far, *near]))
    got = {0: mine[0]}
    for d in SENDS:
        got[d] = toward(mine[d], d)
    for group in GROUPS:
        swapped = swap_cores([got[d][1] for d in group])
        rows = [(got[d], 0) for d in group] + [(swapped, i) for i in range(len(group))]
        out = place([(d, half) for half in range(2) for d in group], rows, out)
    out = out.reshape(2, NV, 1, KL, NLEV, NL)
    return jnp.swapaxes(out, 3, 4)


def solution(mesh):
    fine = Mesh(mesh.devices.reshape(NZ, NC, NX, NH, NY), ("zl", "core", "x", "zh", "y"))
    spec = P(("x", "zh", "y"), ("zl", "core"), None, None, None)
    return jax.shard_map(
        on_device,
        mesh=fine,
        in_specs=(spec, spec),
        out_specs=P(None, None, ("zl", "core"), None, ("x", "zh", "y"), None),
        check_vma=False,
    )
```
